256 devices in a mesh: blk: 64 (over y_lo, x, z), states: 4 (over y_hi, core).
Axes of the slice: x: 4, y: 4 (y_hi: 2, y_lo: 2; y = y_hi * 2 + y_lo), z: 8, core: 2. Of those that a mesh axis runs over, the one named last changes fastest.
Arguments:
- start_states: float32 [128, 16, 128, 512], P('blk', None, None, 'states'), may hold values from -6 to 6
- couplings: float32 [16, 128, 128], replicated, may hold values from -0.1875 to 0.1875
- potential: float32 [128, 16, 128], P('blk'), may hold values from -18 to 18
- site_offsets: int32 [128, 6, 16], P('blk'), may hold values from 0 to 15
- coupling_index: int32 [128, 7, 16], P('blk'), may hold values from 0 to 15
- degrees: int32 [512], P('states'), may hold values from 1 to 3, as said below
Outputs:
- orthonormal: float32 [128, 16, 128, 512], P('blk', 'states')
The draws below stay inside these ranges and needn't reach their ends.
Inputs may be any that keep to these rules, and one draw needn't show every extreme that they name: `degrees`: every degree from 1 to 3 belongs to some state.
All inputs are finite; a program needn't handle non-finite values.
Results may differ from the reference program's by a relative error of at most 0.0003.
Values sent between devices are 32-bit elements; how exact they have to be, the bound alone decides.
A program may use at most 128 MiB of HBM per device.

```python
import jax
import jax.numpy as jnp
from jax import lax

SITES = 16
ORB = 128
S = 512
NC = 16
DEG = 3
LAYERS = 128


def draw_potential(key, part):
    layer_ids = jnp.arange(LAYERS, dtype=jnp.float32)
    amplitude = 6.0 * (1.0 + 2.0 * layer_ids / max(LAYERS - 1, 1))
    base = jax.random.uniform(key, (LAYERS, SITES, ORB), jnp.float32, minval=-1.0, maxval=1.0)
    return (amplitude[:, None, None] * base).astype(jnp.float32)


def draw_degrees(key, part):
    order = jax.random.permutation(key, S)
    return (1 + order % DEG).astype(jnp.int32)


def set_ends(entries, key, least, largest):
    place = [jax.random.randint(jax.random.fold_in(key, axis), (), 0, length) for axis, length in enumerate(entries.shape)]
    widest = entries.shape.index(max(entries.shape))
    beside = place[:widest] + [(place[widest] + 1) % entries.shape[widest]] + place[widest + 1:]
    return entries.at[tuple(place)].set(least).at[tuple(beside)].set(largest)


def levels(rng, extent, split, low, top_value):
    gain, own = 1.0, jax.random.fold_in(rng, 6)
    for position, shards_of in split:
        steps = jnp.exp(jax.random.uniform(jax.random.fold_in(own, position), (shards_of,), jnp.float32, low / len(split), top_value / len(split)))
        gain = gain * jnp.repeat(steps, extent[position] // shards_of).reshape([-1 if axis == position else 1 for axis in range(len(extent))])
    return gain


def bell_draw(rng, extent, spread, limit, cuts=(), held_as=jnp.bfloat16):
    result = spread * jax.random.normal(rng, extent, jnp.float32)
    if cuts:
        result = result * levels(rng, extent, cuts, -0.22, 0.18)
    return jnp.clip(result, -limit, limit).astype(held_as)


def setup_inputs(seed: int = 0) -> dict:
    key_list = jax.random.split(jax.random.key(seed), 7)
    return {
        "start_states": bell_draw(key_list[0], (LAYERS, SITES, ORB, S), 1.0, 6.0, ((0, 64), (3, 4)), jnp.float32),
        "couplings": bell_draw(key_list[1], (NC, ORB, ORB), (7 * ORB) ** -0.5, 0.1875, (), jnp.float32),
        "potential": draw_potential(jax.random.fold_in(key_list[6], 71), 0),
        "site_offsets": set_ends(jax.random.randint(key_list[3], (LAYERS, 6, SITES), 0, SITES), jax.random.fold_in(key_list[3], 1), 0, SITES - 1).astype(jnp.int32),
        "coupling_index": set_ends(jax.random.randint(key_list[4], (LAYERS, 7, SITES), 0, NC), jax.random.fold_in(key_list[4], 1), 0, NC - 1).astype(jnp.int32),
        "degrees": draw_degrees(jax.random.fold_in(key_list[6], 71), 0),
    }


cut_share = 0.3
exact = lax.Precision.HIGHEST

def apply_inner(padded, couplings, onsite, index_rows, offset_rows):
    middle = padded[1:-1]
    lower_layers = padded[:-2]
    upper_layers = padded[2:]
    count = onsite.shape[1]
    site_ids = jnp.arange(count, dtype=jnp.int32)
    layer_ids = jnp.arange(middle.shape[0], dtype=jnp.int32)
    summed = onsite[..., None] * middle
    for slot in range(7):
        if slot == 5:
            source = lower_layers
        elif slot == 6:
            source = upper_layers
        else:
            source = middle
        if slot == 0:
            moved = middle
        else:
            neighbour = ((site_ids[None, :] + offset_rows[:, slot - 1, :]) % count).astype(jnp.int32)
            moved = source[layer_ids[:, None], neighbour]
        blocks_used = jnp.take(couplings, index_rows[:, slot, :], axis=0)
        summed = summed + jnp.einsum('lsij,lsjn->lsin', blocks_used, moved, precision=exact)
    return summed

def reference(start_states, couplings, potential, site_offsets, coupling_index, degrees):
    row_abs = jnp.sum(jnp.abs(couplings), axis=2)
    diag_all = jnp.diagonal(couplings, axis1=1, axis2=2)
    picked_abs = row_abs[coupling_index]
    picked_diag = diag_all[coupling_index[:, 0, :]]
    centers = picked_diag + potential
    radii = picked_abs[:, 0] - jnp.abs(picked_diag) + jnp.sum(picked_abs[:, 1:], axis=1)
    upper = jnp.max(centers + radii)
    lower = jnp.min(centers - radii)
    cut_edge = lower + cut_share * (upper - lower)
    middle_value = (upper + cut_edge) / 2.0
    half_width = (upper - cut_edge) / 2.0

    def wrapped(field):
        return jnp.concatenate([field[-1:], field, field[:1]], axis=0)

    def scaled(applied, field):
        return (applied - middle_value * field) / half_width

    def apply_whole(field):
        return apply_inner(wrapped(field), couplings, potential, coupling_index, site_offsets)
    first_step = scaled(apply_whole(start_states), start_states)
    second = 2.0 * scaled(apply_whole(first_step), first_step) - start_states
    third = 2.0 * scaled(apply_whole(second), second) - first_step
    chosen = jnp.where(degrees == 1, first_step, jnp.where(degrees == 2, second, third))
    rows = chosen.reshape(-1, chosen.shape[-1])
    gram = lax.dot_general(rows.astype(jnp.float32), rows.astype(jnp.float32), (((0,), (0,)), ((), ())), precision=exact, preferred_element_type=jnp.float32)
    factor = jnp.linalg.cholesky(gram)
    identity = jnp.eye(gram.shape[0], dtype=jnp.float32)
    inverse_factor = jax.scipy.linalg.solve_triangular(factor, identity, lower=True)
    orthonormal = jnp.dot(rows.astype(jnp.float32), inverse_factor.T.astype(jnp.float32), precision=exact, preferred_element_type=jnp.float32)
    return orthonormal.reshape(chosen.shape)
```

```python
import functools
import jax
import jax.numpy as jnp
from jax import lax
from jax.experimental import pallas as pl
from jax.experimental.pallas import tpu as pltpu
from jax.sharding import PartitionSpec as P

cut_share = 0.3

MESH = pl.DeviceIdType.MESH
F32 = jnp.float32
BF16 = jnp.bfloat16
exact = lax.Precision.HIGHEST
VMEM_LIMIT = 60 * 1024 * 1024


def place():
    b, st = lax.axis_index("blk"), lax.axis_index("states")
    z = lax.rem(b, 8)
    x = lax.rem(lax.div(b, 8), 4)
    y = lax.div(st, 2) * 2 + lax.div(b, 32)
    return x, y, z, lax.rem(st, 2)


def device(x, y, z, core):
    return ((lax.rem(y, 2) * 4 + x) * 8 + z, lax.div(y, 2) * 2 + core)


def greet(peers):
    barrier = pltpu.get_barrier_semaphore()
    for peer in peers:
        pl.semaphore_signal(barrier, inc=1, device_id=peer, device_id_type=MESH)
    pl.semaphore_wait(barrier, len(peers))


def send(src, dst, send_sem, recv_sem, peer):
    copy = pltpu.make_async_remote_copy(
        src_ref=src, dst_ref=dst, send_sem=send_sem, recv_sem=recv_sem, device_id=peer, device_id_type=MESH
    )
    copy.start()
    return copy


def rows_at(start, size):
    return pl.ds(pl.multiple_of(start, 8), size)


def sum_kernel(g_ref, out_ref, r1, a1, r2, a2, r3, zbuf, gbuf, send_sems, recv_sems):
    x, y, z, core = place()
    core_peer = device(x, y, z, 1 - core)
    x_peers = [device(lax.rem(x + d, 4), y, z, core) for d in (1, 2, 3)]
    y_peers = [device(x, lax.rem(y + d, 4), z, core) for d in (1, 2, 3)]
    z_peers = [device(x, y, lax.rem(z + d, 8), core) for d in range(1, 8)]
    greet([core_peer] + x_peers + y_peers + z_peers)
    used = iter(range(21))

    def sems():
        i = next(used)
        return send_sems.at[i], recv_sems.at[i]

    send(g_ref.at[rows_at((1 - core) * 640, 640)], r1, *sems(), core_peer).wait()
    a1[...] = g_ref[rows_at(core * 640, 640)] + r1[...]
    copies = [
        send(a1.at[rows_at(lax.rem(x + d, 4) * 160, 160)], r2.at[d - 1], *sems(), x_peers[d - 1]) for d in (1, 2, 3)
    ]
    for copy in copies:
        copy.wait()
    a2[...] = (a1[rows_at(x * 160, 160)] + r2[0]) + (r2[1] + r2[2])
    copies = [
        send(a2.at[rows_at(lax.rem(y + d, 4) * 40, 40)], r3.at[d - 1], *sems(), y_peers[d - 1]) for d in (1, 2, 3)
    ]
    for copy in copies:
        copy.wait()
    zbuf[z] = (a2[rows_at(y * 40, 40)] + r3[0]) + (r3[1] + r3[2])
    copies = [send(zbuf.at[z], zbuf.at[z], *sems(), z_peers[d - 1]) for d in range(1, 8)]
    for copy in copies:
        copy.wait()
    own = rows_at(core * 640 + x * 160 + y * 40, 40)
    gbuf[own] = ((zbuf[0] + zbuf[1]) + (zbuf[2] + zbuf[3])) + ((zbuf[4] + zbuf[5]) + (zbuf[6] + zbuf[7]))
    copies = [send(gbuf.at[own], gbuf.at[own], *sems(), peer) for peer in y_peers]
    for copy in copies:
        copy.wait()
    own = rows_at(core * 640 + x * 160, 160)
    copies = [send(gbuf.at[own], gbuf.at[own], *sems(), peer) for peer in x_peers]
    for copy in copies:
        copy.wait()
    own = rows_at(core * 640, 640)
    send(gbuf.at[own], gbuf.at[own], *sems(), core_peer).wait()
    out_ref[...] = gbuf[...]


def sum_over_devices(packed):
    vmem = pl.BlockSpec(memory_space=pltpu.VMEM)
    return pl.pallas_call(
        sum_kernel,
        out_shape=jax.ShapeDtypeStruct((1280, 128), F32),
        in_specs=[vmem],
        out_specs=vmem,
        scratch_shapes=[
            pltpu.VMEM((640, 128), F32),
            pltpu.VMEM((640, 128), F32),
            pltpu.VMEM((3, 160, 128), F32),
            pltpu.VMEM((160, 128), F32),
            pltpu.VMEM((3, 40, 128), F32),
            pltpu.VMEM((8, 40, 128), F32),
            pltpu.VMEM((1280, 128), F32),
            pltpu.SemaphoreType.DMA((21,)),
            pltpu.SemaphoreType.DMA((21,)),
        ],
        compiler_params=pltpu.CompilerParams(collective_id=1, has_side_effects=True),
        name="gram_sum",
    )(packed)


PAIRS = [(i, j) for i in range(4) for j in range(i + 1)]
SLOT = {pair: n for n, pair in enumerate(PAIRS)}


def halves(v):
    hi = v.astype(BF16)
    return hi, (v - hi.astype(F32)).astype(BF16)


def thirds(v):
    hi = v.astype(BF16).astype(F32)
    rest = v - hi
    mid = rest.astype(BF16).astype(F32)
    return hi, mid, rest - mid


def dot_nt(a, b):
    return lax.dot_general(a, b, (((1,), (1,)), ((), ())), precision=exact, preferred_element_type=F32)


def dot_nn(a, b):
    return lax.dot_general(a, b, (((1,), (0,)), ((), ())), precision=exact, preferred_element_type=F32)


def eliminate(work):
    row = lax.broadcasted_iota(jnp.int32, (8, 128), 0)
    for p in range(16):
        lo = 8 * p
        left, right = work[lo : lo + 8, :128], work[lo : lo + 8, 128:]
        cols = [jnp.broadcast_to(left[:, lo + c : lo + c + 1], (8, 128)) for c in range(8)]
        for j in range(8):
            scale = lax.rsqrt(jnp.broadcast_to(cols[j][j : j + 1, :], (8, 128)))
            lrow = jnp.broadcast_to(left[j : j + 1, :], (8, 128)) * scale
            rrow = jnp.broadcast_to(right[j : j + 1, :], (8, 128)) * scale
            factor = jnp.where(row > j, cols[j] * scale, 0.0)
            for c in range(j + 1, 8):
                cols[c] = cols[c] - factor * (jnp.broadcast_to(cols[c][j : j + 1, :], (8, 128)) * scale)
            left = jnp.where(row == j, lrow, left - factor * lrow)
            right = jnp.where(row == j, rrow, right - factor * rrow)
        work[lo : lo + 8, :128] = left
        work[lo : lo + 8, 128:] = right
        if p < 15:
            h, m, l = thirds(jnp.concatenate([left, right], axis=1))
            lhs = jnp.concatenate([h[:, :128], h[:, :128], m[:, :128], m[:, :128], h[:, :128], l[:, :128]], axis=0).astype(BF16)
            rhs = jnp.concatenate([h, m, h, m, l, h], axis=0).astype(BF16)
            change = lax.dot_general(lhs, rhs, (((0,), (0,)), ((), ())), preferred_element_type=F32)
            work[lo + 8 :, :] = work[lo + 8 :, :] - change[lo + 8 :, :]


def factor_kernel(g_ref, x_ref, out_ref, blocks, work, low, inv, xh, xl, ih, il):
    blocks[...] = g_ref[...]
    inv[...] = jnp.zeros_like(inv)
    xh[...], xl[...] = halves(x_ref[...])
    eye = (lax.broadcasted_iota(jnp.int32, (128, 128), 0) == lax.broadcasted_iota(jnp.int32, (128, 128), 1)).astype(F32)

    @pl.loop(0, 4)
    def _(k):
        work[:, :128] = blocks[lax.div(k * (k + 1), 2) + k]
        work[:, 128:] = eye
        eliminate(work)
        for n in range(4):

            @pl.when(k == n)
            def _():
                here = slice(128 * n, 128 * n + 128)
                w = work[:, 128:]
                inv[here, here] = w
                if n > 0:
                    known = dot_nn(low[here, : 128 * n], inv[: 128 * n, : 128 * n])
                    inv[here, : 128 * n] = -dot_nn(w, known)
                for i in range(n + 1, 4):
                    low[128 * i : 128 * i + 128, here] = dot_nt(blocks[SLOT[i, n]], w)
                for j in range(n + 1, 4):
                    for i in range(j, 4):
                        blocks[SLOT[i, j]] = blocks[SLOT[i, j]] - dot_nt(
                            low[128 * i : 128 * i + 128, here], low[128 * j : 128 * j + 128, here]
                        )

    ih[...], il[...] = halves(inv[...])

    def nt(a, b):
        return lax.dot_general(a, b, (((1,), (1,)), ((), ())), preferred_element_type=F32)

    for i in range(4):
        here, upto = slice(128 * i, 128 * i + 128), 128 * i + 128
        a, b = xh[:, :upto], xl[:, :upto]
        u, v = ih[here, :upto], il[here, :upto]
        out_ref[:, here] = nt(a, u) + (nt(a, v) + nt(b, u))


def orthonormalised(packed, rows):
    vmem = pl.BlockSpec(memory_space=pltpu.VMEM)
    return pl.pallas_call(
        factor_kernel,
        out_shape=jax.ShapeDtypeStruct((1024, 512), F32),
        in_specs=[vmem, vmem],
        out_specs=vmem,
        scratch_shapes=[
            pltpu.VMEM((10, 128, 128), F32),
            pltpu.VMEM((128, 256), F32),
            pltpu.VMEM((512, 512), F32),
            pltpu.VMEM((512, 512), F32),
            pltpu.VMEM((1024, 512), BF16),
            pltpu.VMEM((1024, 512), BF16),
            pltpu.VMEM((512, 512), BF16),
            pltpu.VMEM((512, 512), BF16),
        ],
        compiler_params=pltpu.CompilerParams(vmem_limit_bytes=VMEM_LIMIT),
        name="factor",
    )(packed.reshape(10, 128, 128), rows)


def padded_2(shard, sides, width):
    for axis, dim in sides:
        devices, length = (lax.axis_size(axis), shard.shape[dim])
        up = [(i, (i + 1) % devices) for i in range(devices)]
        down = [(j, i) for i, j in up]
        last = lax.slice_in_dim(shard, length - width, length, axis=dim)
        first = lax.slice_in_dim(shard, 0, width, axis=dim)
        before = lax.ppermute(last, axis, up)
        after = lax.ppermute(first, axis, down)
        shard = jnp.concatenate([before, shard, after], axis=dim)
    return shard


def copy_for_each(shard, axis):
    copies = jnp.broadcast_to(shard, (lax.axis_size(axis), *shard.shape))
    return lax.all_to_all(copies, axis, split_axis=0, concat_axis=0, tiled=True)


def folded_in_pairs(pieces, combine):
    while len(jax.tree.leaves(pieces)[0]) > 1:
        pieces = jax.vmap(combine)(
            *(jax.tree.map(lambda part: part[side::2], pieces) for side in (0, 1))
        )
    return jax.tree.map(lambda part: part[0], pieces)


def joined_all(shard, axis, combine):
    pieces = jax.tree.map(lambda part: copy_for_each(part, axis), shard)
    return folded_in_pairs(pieces, combine)


def coupling_blocks(couplings, index_rows):
    return jnp.take(couplings, index_rows, axis=0)


def apply_inner(padded, blocks_used, onsite, offset_rows):
    middle = padded[1:-1]
    lower_layers = padded[:-2]
    upper_layers = padded[2:]
    count = onsite.shape[1]
    site_ids = jnp.arange(count, dtype=jnp.int32)
    layer_ids = jnp.arange(middle.shape[0], dtype=jnp.int32)
    pieces = [middle]
    for slot in range(1, 7):
        if slot == 5:
            source = lower_layers
        elif slot == 6:
            source = upper_layers
        else:
            source = middle
        neighbour = (site_ids[None, :] + offset_rows[:, slot - 1, :]) % count
        pieces.append(source[layer_ids[:, None], neighbour])
    stacked = jnp.stack(pieces, axis=1)
    summed = jnp.einsum("lksij,lksjn->lsin", blocks_used, stacked, precision=exact)
    return summed + onsite[..., None] * middle


def extrema_of(couplings, onsite, index_rows):
    row_abs = jnp.sum(jnp.abs(couplings), axis=2)
    diag_all = jnp.diagonal(couplings, axis1=1, axis2=2)
    table_ids = jnp.arange(couplings.shape[0], dtype=jnp.int32)
    onehot = (index_rows[..., None] == table_ids).astype(jnp.float32)
    picked_abs = jnp.einsum("lksc,ci->lksi", onehot, row_abs, precision=exact)
    picked_diag = jnp.einsum("lsc,ci->lsi", onehot[:, 0], diag_all, precision=exact)
    centers = picked_diag + onsite
    radii = picked_abs[:, 0] - jnp.abs(picked_diag) + jnp.sum(picked_abs[:, 1:], axis=1)
    return (jnp.max(centers + radii), jnp.min(centers - radii))


def combine(first, second):
    return (jnp.maximum(first[0], second[0]), jnp.minimum(first[1], second[1]))


def faces(field):
    return padded_2(field, (("blk", 0),), 1)


def per_device(start_states, couplings, potential, site_offsets, coupling_index, degrees):
    upper, lower = joined_all(extrema_of(couplings, potential, coupling_index), "blk", combine)
    cut_edge = lower + cut_share * (upper - lower)
    middle_value = (upper + cut_edge) / 2.0
    half_width = (upper - cut_edge) / 2.0

    def scaled(applied, field):
        return (applied - middle_value * field) / half_width

    local_blocks = coupling_blocks(couplings, coupling_index)
    first_step = scaled(
        apply_inner(faces(start_states), local_blocks, potential, site_offsets), start_states
    )
    second = (
        2.0
        * scaled(apply_inner(faces(first_step), local_blocks, potential, site_offsets), first_step)
        - start_states
    )
    third = (
        2.0 * scaled(apply_inner(faces(second), local_blocks, potential, site_offsets), second)
        - first_step
    )
    chosen = jnp.where(degrees == 1, first_step, jnp.where(degrees == 2, second, third))
    regrouped = lax.all_to_all(chosen, "states", split_axis=1, concat_axis=3, tiled=True)
    rows = regrouped.reshape(-1, regrouped.shape[-1])
    partial_gram = lax.dot_general(
        rows, rows, (((0,), (0,)), ((), ())), precision=exact, preferred_element_type=jnp.float32
    )
    packed = jnp.concatenate(
        [partial_gram[128 * i : 128 * i + 128, 128 * j : 128 * j + 128] for i, j in PAIRS], axis=0
    )
    gram = sum_over_devices(packed)
    return orthonormalised(gram, rows).reshape(regrouped.shape)


def solution(mesh):
    in_specs = (
        P("blk", None, None, "states"),
        P(),
        P("blk", None, None),
        P("blk", None, None),
        P("blk", None, None),
        P("states"),
    )
    out_specs = P("blk", "states", None, None)
    return jax.shard_map(
        per_device, mesh=mesh, in_specs=in_specs, out_specs=out_specs, check_vma=False
    )
```

```python
import jax
import jax.numpy as jnp
from jax import lax
from jax.experimental import pallas as pl
from jax.experimental.pallas import tpu as pltpu
from jax.sharding import PartitionSpec as P

cut_share = 0.3

MESH = pl.DeviceIdType.MESH
F32 = jnp.float32
BF16 = jnp.bfloat16
exact = lax.Precision.HIGHEST
VMEM_LIMIT = 60 * 1024 * 1024


def place():
    b, st = lax.axis_index("blk"), lax.axis_index("states")
    z = lax.rem(b, 8)
    x = lax.rem(lax.div(b, 8), 4)
    y = lax.div(st, 2) * 2 + lax.div(b, 32)
    return x, y, z, lax.rem(st, 2)


def device(x, y, z, core):
    return ((lax.rem(y, 2) * 4 + x) * 8 + z, lax.div(y, 2) * 2 + core)


def send(src, dst, send_sem, recv_sem, peer):
    copy = pltpu.make_async_remote_copy(
        src_ref=src, dst_ref=dst, send_sem=send_sem, recv_sem=recv_sem, device_id=peer, device_id_type=MESH
    )
    copy.start()
    return copy


def rows_at(start, size):
    return pl.ds(pl.multiple_of(start, 8), size)


def nt(a, b):
    return lax.dot_general(a, b, (((1,), (1,)), ((), ())), preferred_element_type=F32)


def sum_kernel(xt_ref, out_ref, xh_ref, xl_ref, hi, lo, g_ref, r1, a1, r2, a2, r3, zbuf, gbuf, send_sems, recv_sems):
    x, y, z, core = place()
    core_peer = device(x, y, z, 1 - core)
    x_peers = [device(lax.rem(x + d, 4), y, z, core) for d in (1, 2, 3)]
    y_peers = [device(x, lax.rem(y + d, 4), z, core) for d in (1, 2, 3)]
    z_peers = [device(x, y, lax.rem(z + d, 8), core) for d in range(1, 8)]
    peers = [core_peer] + x_peers + y_peers + z_peers
    barrier = pltpu.get_barrier_semaphore()
    for peer in peers:
        pl.semaphore_signal(barrier, inc=1, device_id=peer, device_id_type=MESH)
    for q in range(8):
        cols = slice(128 * q, 128 * q + 128)
        hi[:, cols], lo[:, cols] = halves(xt_ref[q])
    for i in range(4):
        here, upto = slice(128 * i, 128 * i + 128), 128 * i + 128
        block = nt(hi[here], hi[:upto]) + (nt(hi[here], lo[:upto]) + nt(lo[here], hi[:upto]))
        for j in range(i + 1):
            g_ref[128 * SLOT[i, j] : 128 * SLOT[i, j] + 128] = block[:, 128 * j : 128 * j + 128]
    pl.semaphore_wait(barrier, len(peers))
    used = iter(range(21))

    def sems():
        i = next(used)
        return send_sems.at[i], recv_sems.at[i]

    copy = send(g_ref.at[rows_at((1 - core) * 640, 640)], r1, *sems(), core_peer)
    copy.wait()
    a1[...] = g_ref[rows_at(core * 640, 640)] + r1[...]
    copies = [
        send(a1.at[rows_at(lax.rem(x + d, 4) * 160, 160)], r2.at[d - 1], *sems(), x_peers[d - 1]) for d in (1, 2, 3)
    ]

    @pl.loop(0, 8)
    def _(q):
        at = pl.ds(pl.multiple_of((lax.rem(q, 2) * 4 + lax.div(q, 2)) * 128, 128), 128)
        for d in range(4):
            cols = slice(128 * d, 128 * d + 128)
            xh_ref[at, cols], xl_ref[at, cols] = halves(xt_ref[q, cols].T)

    for copy in copies:
        copy.wait()
    a2[...] = (a1[rows_at(x * 160, 160)] + r2[0]) + (r2[1] + r2[2])
    copies = [
        send(a2.at[rows_at(lax.rem(y + d, 4) * 40, 40)], r3.at[d - 1], *sems(), y_peers[d - 1]) for d in (1, 2, 3)
    ]
    for copy in copies:
        copy.wait()
    zbuf[z] = (a2[rows_at(y * 40, 40)] + r3[0]) + (r3[1] + r3[2])
    copies = [send(zbuf.at[z], zbuf.at[z], *sems(), z_peers[d - 1]) for d in range(1, 8)]
    for copy in copies:
        copy.wait()
    own = rows_at(core * 640 + x * 160 + y * 40, 40)
    gbuf[own] = ((zbuf[0] + zbuf[1]) + (zbuf[2] + zbuf[3])) + ((zbuf[4] + zbuf[5]) + (zbuf[6] + zbuf[7]))
    copies = [send(gbuf.at[own], gbuf.at[own], *sems(), peer) for peer in y_peers]
    for copy in copies:
        copy.wait()
    own = rows_at(core * 640 + x * 160, 160)
    copies = [send(gbuf.at[own], gbuf.at[own], *sems(), peer) for peer in x_peers]
    for copy in copies:
        copy.wait()
    own = rows_at(core * 640, 640)
    send(gbuf.at[own], gbuf.at[own], *sems(), core_peer).wait()
    out_ref[...] = gbuf[...]


def gram_over_devices(xt):
    vmem = pl.BlockSpec(memory_space=pltpu.VMEM)
    return pl.pallas_call(
        sum_kernel,
        out_shape=[
            jax.ShapeDtypeStruct((1280, 128), F32),
            jax.ShapeDtypeStruct((1024, 512), BF16),
            jax.ShapeDtypeStruct((1024, 512), BF16),
        ],
        in_specs=[vmem],
        out_specs=[vmem] * 3,
        scratch_shapes=[
            pltpu.VMEM((512, 1024), BF16),
            pltpu.VMEM((512, 1024), BF16),
            pltpu.VMEM((1280, 128), F32),
            pltpu.VMEM((640, 128), F32),
            pltpu.VMEM((640, 128), F32),
            pltpu.VMEM((3, 160, 128), F32),
            pltpu.VMEM((160, 128), F32),
            pltpu.VMEM((3, 40, 128), F32),
            pltpu.VMEM((8, 40, 128), F32),
            pltpu.VMEM((1280, 128), F32),
            pltpu.SemaphoreType.DMA((21,)),
            pltpu.SemaphoreType.DMA((21,)),
        ],
        compiler_params=pltpu.CompilerParams(collective_id=1, has_side_effects=True, vmem_limit_bytes=VMEM_LIMIT),
        name="gram_sum",
    )(xt.reshape(8, 512, 128))


PAIRS = [(i, j) for i in range(4) for j in range(i + 1)]
SLOT = {pair: n for n, pair in enumerate(PAIRS)}


def halves(v):
    hi = v.astype(BF16)
    return hi, (v - hi.astype(F32)).astype(BF16)


def thirds(v):
    hi = v.astype(BF16).astype(F32)
    rest = v - hi
    mid = rest.astype(BF16).astype(F32)
    return hi, mid, rest - mid


def dot_nt(a, b):
    return lax.dot_general(a, b, (((1,), (1,)), ((), ())), precision=exact, preferred_element_type=F32)


def dot_nn(a, b):
    return lax.dot_general(a, b, (((1,), (0,)), ((), ())), precision=exact, preferred_element_type=F32)


def eliminate(work):
    row = lax.broadcasted_iota(jnp.int32, (8, 128), 0)
    for p in range(16):
        lo = 8 * p
        left, right = work[lo : lo + 8, :128], work[lo : lo + 8, 128:]
        cols = [jnp.broadcast_to(left[:, lo + c : lo + c + 1], (8, 128)) for c in range(8)]
        for j in range(8):
            scale = lax.rsqrt(jnp.broadcast_to(cols[j][j : j + 1, :], (8, 128)))
            lrow = jnp.broadcast_to(left[j : j + 1, :], (8, 128)) * scale
            rrow = jnp.broadcast_to(right[j : j + 1, :], (8, 128)) * scale
            factor = jnp.where(row > j, cols[j] * scale, 0.0)
            for c in range(j + 1, 8):
                cols[c] = cols[c] - factor * (jnp.broadcast_to(cols[c][j : j + 1, :], (8, 128)) * scale)
            left = jnp.where(row == j, lrow, left - factor * lrow)
            right = jnp.where(row == j, rrow, right - factor * rrow)
        work[lo : lo + 8, :128] = left
        work[lo : lo + 8, 128:] = right
        if p < 15:
            h, m, l = thirds(jnp.concatenate([left, right], axis=1))
            lhs = jnp.concatenate([h[:, :128], h[:, :128], m[:, :128], m[:, :128], h[:, :128], l[:, :128]], axis=0).astype(BF16)
            rhs = jnp.concatenate([h, m, h, m, l, h], axis=0).astype(BF16)
            change = lax.dot_general(lhs, rhs, (((0,), (0,)), ((), ())), preferred_element_type=F32)
            work[lo + 8 :, :] = work[lo + 8 :, :] - change[lo + 8 :, :]


def factor_kernel(g_ref, xh, xl, out_ref, blocks, work, low, inv, ih, il):
    blocks[...] = g_ref[...]
    inv[...] = jnp.zeros_like(inv)
    eye = (lax.broadcasted_iota(jnp.int32, (128, 128), 0) == lax.broadcasted_iota(jnp.int32, (128, 128), 1)).astype(F32)

    @pl.loop(0, 4)
    def _(k):
        work[:, :128] = blocks[lax.div(k * (k + 1), 2) + k]
        work[:, 128:] = eye
        eliminate(work)
        for n in range(4):

            @pl.when(k == n)
            def _():
                here = slice(128 * n, 128 * n + 128)
                w = work[:, 128:]
                inv[here, here] = w
                if n > 0:
                    known = dot_nn(low[here, : 128 * n], inv[: 128 * n, : 128 * n])
                    inv[here, : 128 * n] = -dot_nn(w, known)
                for i in range(n + 1, 4):
                    low[128 * i : 128 * i + 128, here] = dot_nt(blocks[SLOT[i, n]], w)
                for j in range(n + 1, 4):
                    for i in range(j, 4):
                        blocks[SLOT[i, j]] = blocks[SLOT[i, j]] - dot_nt(
                            low[128 * i : 128 * i + 128, here], low[128 * j : 128 * j + 128, here]
                        )

    ih[...], il[...] = halves(inv[...])

    for i in range(4):
        here, upto = slice(128 * i, 128 * i + 128), 128 * i + 128
        a, b = xh[:, :upto], xl[:, :upto]
        u, v = ih[here, :upto], il[here, :upto]
        out_ref[:, here] = nt(a, u) + (nt(a, v) + nt(b, u))


def orthonormalised(packed, xh, xl):
    vmem = pl.BlockSpec(memory_space=pltpu.VMEM)
    return pl.pallas_call(
        factor_kernel,
        out_shape=jax.ShapeDtypeStruct((1024, 512), F32),
        in_specs=[vmem] * 3,
        out_specs=vmem,
        scratch_shapes=[
            pltpu.VMEM((10, 128, 128), F32),
            pltpu.VMEM((128, 256), F32),
            pltpu.VMEM((512, 512), F32),
            pltpu.VMEM((512, 512), F32),
            pltpu.VMEM((512, 512), BF16),
            pltpu.VMEM((512, 512), BF16),
        ],
        compiler_params=pltpu.CompilerParams(vmem_limit_bytes=VMEM_LIMIT),
        name="factor",
    )(packed.reshape(10, 128, 128), xh, xl)


NCH = 2
WIDTH = 128 // NCH


def both_halves(v):
    hi, lo = halves(v)
    return jnp.concatenate([hi, lo], axis=0)


def product(lhs, rhs):
    full = lax.dot_general(lhs, rhs, (((1,), (0,)), ((), ())), preferred_element_type=F32)
    return (full[:WIDTH, :128] + full[WIDTH:, :128]) + (full[:WIDTH, 128:] + full[WIDTH:, 128:])


def filter_kernel(index_ref, offset_ref, start_ref, coup_ref, pot_ref, deg_ref, xt_ref, *scratch):
    scratch = iter(scratch)
    field = [[next(scratch) for _ in range(NCH)] for _ in range(3)]
    stack = [[next(scratch) for _ in range(NCH)] for _ in range(3)]
    halo = [[[next(scratch) for _ in range(2)] for _ in range(NCH)] for _ in range(3)]
    partial = next(scratch)
    chosen = [next(scratch) for _ in range(NCH)]
    blocks, row_abs, diag = next(scratch), next(scratch), next(scratch)
    zb, xb, yb = next(scratch), next(scratch), next(scratch)
    degree = next(scratch)
    send_sems, recv_sems = next(scratch), next(scratch)
    used = iter(range(12 * NCH + 11))

    def sems():
        i = next(used)
        return send_sems.at[i], recv_sems.at[i]

    b, st = lax.axis_index("blk"), lax.axis_index("states")
    z, xx, ylo = lax.rem(b, 8), lax.rem(lax.div(b, 8), 4), lax.div(b, 32)
    left, right = (lax.rem(b + 63, 64), st), (lax.rem(b + 1, 64), st)
    z_peers = [(b - z + lax.rem(z + d, 8), st) for d in range(1, 8)]
    x_peers = [(b - xx * 8 + lax.rem(xx + d, 4) * 8, st) for d in range(1, 4)]
    y_peer = (lax.rem(b + 32, 64), st)
    state_peers = [(b, lax.rem(st + d, 4)) for d in range(1, 4)]
    peers = [left, right, y_peer] + z_peers + x_peers + state_peers
    barrier = pltpu.get_barrier_semaphore()
    for peer in peers:
        pl.semaphore_signal(barrier, inc=1, device_id=peer, device_id_type=MESH)

    @pl.loop(0, 16)
    def _(s):
        for l in range(2):
            turned = start_ref[l, s].T
            for c in range(NCH):
                part = turned[WIDTH * c : WIDTH * c + WIDTH]
                field[0][c][l, s] = part
                stack[0][c][l, s] = both_halves(part)

    pl.semaphore_wait(barrier, len(peers))
    copies = []
    edge = {}

    def send_edge(k, c, l):
        source = field[k][c].at[l]
        copy = send(source, halo[k][c][1 - l], *sems(), right if l else left)
        copies.append(copy)
        edge[k, c, 1 - l] = copy

    for c in range(NCH):
        send_edge(0, c, 0)
        send_edge(0, c, 1)

    eye = lax.broadcasted_iota(jnp.int32, (128, 128), 0) == lax.broadcasted_iota(jnp.int32, (128, 128), 1)

    @pl.loop(0, 16)
    def _(n):
        turned = coup_ref[n].T
        row_abs[pl.ds(n, 1)] = jnp.sum(jnp.abs(turned), axis=0, keepdims=True)
        diag[pl.ds(n, 1)] = jnp.sum(jnp.where(eye, turned, 0.0), axis=0, keepdims=True)
        blocks[n] = jnp.concatenate(halves(turned), axis=1)

    def bounds_of(s, ends):
        top, low = ends
        for l in range(2):
            first = index_ref[l, 0, s]
            middle = diag[pl.ds(first, 1)]
            center = middle + pot_ref[l, pl.ds(s, 1)]
            radius = row_abs[pl.ds(first, 1)] - jnp.abs(middle)
            rest = row_abs[pl.ds(index_ref[l, 1, s], 1)]
            for slot in range(2, 7):
                rest = rest + row_abs[pl.ds(index_ref[l, slot, s], 1)]
            radius = radius + rest
            top = jnp.maximum(top, center + radius)
            low = jnp.maximum(low, radius - center)
        return top, low

    least = jnp.full((1, 128), -3e38, F32)
    top, low = lax.fori_loop(0, 16, bounds_of, (least, least))
    zb[z] = jnp.concatenate([jnp.broadcast_to(top, (8, 128)), jnp.broadcast_to(low, (8, 128))], axis=0)

    def exchange(buf, at, group):
        started = [send(buf.at[at], buf.at[at], *sems(), peer) for peer in group]
        copies.extend(started)
        return started

    def merged(buf, started):
        for copy in started:
            copy.wait_recv()
        best = buf[0]
        for i in range(1, buf.shape[0]):
            best = jnp.maximum(best, buf[i])
        return best

    def local_part(k, c):
        @pl.loop(0, 16)
        def _(s):
            for l in range(2):
                sources = [(l, s)]
                for slot in range(1, 5):
                    sources.append((l, (s + offset_ref[l, slot - 1, s]) & 15))
                slots = [0, 1, 2, 3, 4, 6 - l]
                sources.append((1 - l, (s + offset_ref[l, 5 - l, s]) & 15))
                lhs = jnp.concatenate([stack[k][c][at] for at in sources], axis=1)
                rhs = jnp.concatenate([blocks[index_ref[l, slot, s]] for slot in slots], axis=0)
                partial[l, s] = product(lhs, rhs)

    def finish(k, c, middle, inverse):
        for l in range(2):
            edge[k, c, l].wait_recv()

            @pl.loop(0, 16)
            def _(s):
                slot = 5 + l
                outer = halo[k][c][l][(s + offset_ref[l, slot - 1, s]) & 15]
                total = partial[l, s] + product(both_halves(outer), blocks[index_ref[l, slot, s]])
                own = field[k][c][l, s]
                new = (total + (pot_ref[l, pl.ds(s, 1)] - middle) * own) * inverse
                if k > 0:
                    new = 2.0 * new - field[k - 1][c][l, s]
                if k < 2:
                    field[k + 1][c][l, s] = new
                    stack[k + 1][c][l, s] = both_halves(new)
                else:
                    d = degree[WIDTH * c : WIDTH * c + WIDTH]
                    chosen[c][s, l] = jnp.where(d == 1, field[1][c][l, s], jnp.where(d == 2, own, new))

            if k < 2:
                send_edge(k + 1, c, l)

    started = exchange(zb, z, z_peers)
    degree[...] = jnp.broadcast_to(deg_ref[...].astype(F32), (128, 128)).T.astype(jnp.int32)
    local_part(0, 0)
    xb[xx] = merged(zb, started)
    started = exchange(xb, xx, x_peers)
    best = merged(xb, started)
    yb[ylo] = best
    started = exchange(yb, ylo, [y_peer])
    best = merged(yb, started)
    upper = jnp.max(best[:8], axis=1, keepdims=True)[:1]
    lower = -jnp.max(best[8:], axis=1, keepdims=True)[:1]
    cut_edge = lower + cut_share * (upper - lower)
    middle = jnp.broadcast_to((upper + cut_edge) / 2.0, (1, 128))
    inverse = jnp.broadcast_to(2.0 / (upper - cut_edge), (1, 128))

    arrivals = []
    for k in range(3):
        for c in range(NCH):
            if (k, c) != (0, 0):
                local_part(k, c)
            finish(k, c, middle, inverse)
            if k == 2:
                rows = pl.ds(pl.multiple_of(128 * st + WIDTH * c, WIDTH), WIDTH)
                for d in (1, 2, 3):
                    other = lax.rem(st + d, 4)
                    copy = send(
                        chosen[c].at[pl.ds(4 * other, 4)], xt_ref.at[:, :, rows], *sems(), state_peers[d - 1]
                    )
                    copies.append(copy)
                    arrivals.append(copy)
                for s in range(4):
                    for l in range(2):
                        xt_ref[s, l, rows] = chosen[c][4 * st + s, l]
    for copy in arrivals:
        copy.wait_recv()
    for copy in copies:
        copy.wait_send()


def filtered_rows(start_states, couplings, potential, site_offsets, coupling_index, degrees):
    vmem, smem = pl.BlockSpec(memory_space=pltpu.VMEM), pl.BlockSpec(memory_space=pltpu.SMEM)
    scratch = [pltpu.VMEM((2, 16, WIDTH, 128), F32)] * (3 * NCH)
    scratch += [pltpu.VMEM((2, 16, 2 * WIDTH, 128), BF16)] * (3 * NCH)
    scratch += [pltpu.VMEM((16, WIDTH, 128), F32)] * (6 * NCH)
    scratch += [pltpu.VMEM((2, 16, WIDTH, 128), F32)]
    scratch += [pltpu.VMEM((16, 2, WIDTH, 128), F32)] * NCH
    scratch += [pltpu.VMEM((16, 128, 256), BF16), pltpu.VMEM((16, 128), F32), pltpu.VMEM((16, 128), F32)]
    scratch += [pltpu.VMEM((n, 16, 128), F32) for n in (8, 4, 2)]
    scratch += [pltpu.VMEM((128, 128), jnp.int32)]
    scratch += [pltpu.SemaphoreType.DMA((12 * NCH + 11,))] * 2
    return pl.pallas_call(
        filter_kernel,
        out_shape=jax.ShapeDtypeStruct((4, 2, 512, 128), F32),
        in_specs=[smem, smem, vmem, vmem, vmem, vmem],
        out_specs=vmem,
        scratch_shapes=scratch,
        compiler_params=pltpu.CompilerParams(collective_id=0, has_side_effects=True, vmem_limit_bytes=VMEM_LIMIT),
        name="filter",
    )(coupling_index, site_offsets, start_states, couplings, potential, degrees.reshape(1, 128))


def per_device(start_states, couplings, potential, site_offsets, coupling_index, degrees):
    xt = filtered_rows(start_states, couplings, potential, site_offsets, coupling_index, degrees)
    gram, xh, xl = gram_over_devices(xt)
    return orthonormalised(gram, xh, xl).reshape(2, 4, 128, 512)


def solution(mesh):
    in_specs = (
        P("blk", None, None, "states"),
        P(),
        P("blk", None, None),
        P("blk", None, None),
        P("blk", None, None),
        P("states"),
    )
    out_specs = P("blk", "states", None, None)
    return jax.shard_map(
        per_device, mesh=mesh, in_specs=in_specs, out_specs=out_specs, check_vma=False
    )
```

```python
import jax
import jax.numpy as jnp
from jax import lax
from jax.experimental import pallas as pl
from jax.experimental.pallas import tpu as pltpu
from jax.sharding import PartitionSpec as P

cut_share = 0.3

MESH = pl.DeviceIdType.MESH
F32 = jnp.float32
BF16 = jnp.bfloat16
exact = lax.Precision.HIGHEST
VMEM_LIMIT = 60 * 1024 * 1024


def place():
    b, st = lax.axis_index("blk"), lax.axis_index("states")
    z = lax.rem(b, 8)
    x = lax.rem(lax.div(b, 8), 4)
    y = lax.div(st, 2) * 2 + lax.div(b, 32)
    return x, y, z, lax.rem(st, 2)


def device(x, y, z, core):
    return ((lax.rem(y, 2) * 4 + x) * 8 + z, lax.div(y, 2) * 2 + core)


def send(src, dst, send_sem, recv_sem, peer):
    copy = pltpu.make_async_remote_copy(
        src_ref=src, dst_ref=dst, send_sem=send_sem, recv_sem=recv_sem, device_id=peer, device_id_type=MESH
    )
    copy.start()
    return copy


def rows_at(start, size):
    return pl.ds(pl.multiple_of(start, 8), size)


def nt(a, b):
    return lax.dot_general(a, b, (((1,), (1,)), ((), ())), preferred_element_type=F32)


PAIRS = [(i, j) for i in range(4) for j in range(i + 1)]
SLOT = {pair: n for n, pair in enumerate(PAIRS)}


def halves(v):
    hi = v.astype(BF16)
    return hi, (v - hi.astype(F32)).astype(BF16)


def thirds(v):
    hi = v.astype(BF16).astype(F32)
    rest = v - hi
    mid = rest.astype(BF16).astype(F32)
    return hi, mid, rest - mid


def dot_nt(a, b):
    h, m, l = thirds(a)
    u, v, w = thirds(b)
    lhs = jnp.concatenate([h, h, m, m, h, l], axis=1).astype(BF16)
    rhs = jnp.concatenate([u, v, u, v, w, u], axis=1).astype(BF16)
    return lax.dot_general(lhs, rhs, (((1,), (1,)), ((), ())), preferred_element_type=F32)


def dot_nn(a, b):
    h, m, l = thirds(a)
    u, v, w = thirds(b)
    lhs = jnp.concatenate([h, h, m, m, h, l], axis=1).astype(BF16)
    rhs = jnp.concatenate([u, v, u, v, w, u], axis=0).astype(BF16)
    return lax.dot_general(lhs, rhs, (((1,), (0,)), ((), ())), preferred_element_type=F32)


def eliminate(work):
    row = lax.broadcasted_iota(jnp.int32, (16, 128), 0)

    def spread(v, rows=16):
        return jnp.broadcast_to(v, (rows, 128))

    def steps(lo, count):
        left, right = work[lo : lo + 16, :128], work[lo : lo + 16, 128:]
        cols = [spread(left[:, lo + c : lo + c + 1]) for c in range(16)]
        below = []
        for t in range(1, count):
            l2, r2 = work[lo + 16 * t : lo + 16 * t + 16, :128], work[lo + 16 * t : lo + 16 * t + 16, 128:]
            below.append([l2, r2, [spread(l2[:, lo + c : lo + c + 1]) for c in range(16)]])
        for j in range(16):
            scale = lax.rsqrt(jnp.broadcast_to(cols[j][j : j + 1, :], (8, 128)))
            scale = jnp.concatenate([scale] * 2, axis=0)
            factor = jnp.where(row > j, cols[j] * scale, 0.0)
            lrow = spread(left[j : j + 1, :]) * scale
            rrow = spread(right[j : j + 1, :]) * scale
            lower = [part[2][j] * scale for part in below]
            for c in range(j + 1, 16):
                across = spread(cols[c][j : j + 1, :]) * scale
                cols[c] = cols[c] - factor * across
                for part, f in zip(below, lower):
                    part[2][c] = part[2][c] - f * across
            left = jnp.where(row == j, lrow, left - factor * lrow)
            right = jnp.where(row == j, rrow, right - factor * rrow)
            for part, f in zip(below, lower):
                part[0] = part[0] - f * lrow
                part[1] = part[1] - f * rrow
        work[lo : lo + 16, :128] = left
        work[lo : lo + 16, 128:] = right
        for t in range(1, count):
            work[lo + 16 * t : lo + 16 * t + 16, :128] = below[t - 1][0]
            work[lo + 16 * t : lo + 16 * t + 16, 128:] = below[t - 1][1]

    for p in range(128 // PANEL):
        lo = PANEL * p
        for t in range(PANEL // 16):
            steps(lo + 16 * t, PANEL // 16 - t)
        if lo + PANEL < 128:
            h, m, l = thirds(work[lo : lo + PANEL, :])
            lhs = jnp.concatenate([h[:, :128], h[:, :128], m[:, :128], m[:, :128], h[:, :128], l[:, :128]], axis=0).astype(BF16)
            rhs = jnp.concatenate([h, m, h, m, l, h], axis=0).astype(BF16)
            change = lax.dot_general(lhs, rhs, (((0,), (0,)), ((), ())), preferred_element_type=F32)
            work[lo + PANEL :, :] = work[lo + PANEL :, :] - change[lo + PANEL :, :]


PANEL = 32


def factor_kernel(g_ref, xh, xl, out_ref, blocks, work, low, inv, ih, il):
    blocks[...] = g_ref[...]
    inv[...] = jnp.zeros_like(inv)
    eye = (lax.broadcasted_iota(jnp.int32, (128, 128), 0) == lax.broadcasted_iota(jnp.int32, (128, 128), 1)).astype(F32)

    @pl.loop(0, 4)
    def _(k):
        work[:, :128] = blocks[lax.div(k * (k + 1), 2) + k]
        work[:, 128:] = eye
        eliminate(work)
        for n in range(4):

            @pl.when(k == n)
            def _():
                here = slice(128 * n, 128 * n + 128)
                w = work[:, 128:]
                inv[here, here] = w
                if n > 0:
                    known = dot_nn(low[here, : 128 * n], inv[: 128 * n, : 128 * n])
                    inv[here, : 128 * n] = -dot_nn(w, known)
                for i in range(n + 1, 4):
                    low[128 * i : 128 * i + 128, here] = dot_nt(blocks[SLOT[i, n]], w)
                for j in range(n + 1, 4):
                    for i in range(j, 4):
                        blocks[SLOT[i, j]] = blocks[SLOT[i, j]] - dot_nt(
                            low[128 * i : 128 * i + 128, here], low[128 * j : 128 * j + 128, here]
                        )

    ih[...], il[...] = halves(inv[...])

    for i in range(4):
        here, upto = slice(128 * i, 128 * i + 128), 128 * i + 128
        a, b = xh[:, :upto], xl[:, :upto]
        u, v = ih[here, :upto], il[here, :upto]
        out_ref[:, here] = nt(a, u) + (nt(a, v) + nt(b, u))


def orthonormalised(packed, xh, xl):
    vmem = pl.BlockSpec(memory_space=pltpu.VMEM)
    return pl.pallas_call(
        factor_kernel,
        out_shape=jax.ShapeDtypeStruct((1024, 512), F32),
        in_specs=[vmem] * 3,
        out_specs=vmem,
        scratch_shapes=[
            pltpu.VMEM((10, 128, 128), F32),
            pltpu.VMEM((128, 256), F32),
            pltpu.VMEM((512, 512), F32),
            pltpu.VMEM((512, 512), F32),
            pltpu.VMEM((512, 512), BF16),
            pltpu.VMEM((512, 512), BF16),
        ],
        compiler_params=pltpu.CompilerParams(vmem_limit_bytes=VMEM_LIMIT),
        name="factor",
    )(packed.reshape(10, 128, 128), xh, xl)


NCH = 2
WIDTH = 128 // NCH
COPIES = 6 * NCH + 3 * NCH + 9 + 11 + 33


def both_halves(v):
    hi, lo = halves(v)
    return jnp.concatenate([hi, lo], axis=0)


def product(lhs, rhs):
    full = lax.dot_general(lhs, rhs, (((1,), (0,)), ((), ())), preferred_element_type=F32)
    return (full[:WIDTH, :128] + full[WIDTH:, :128]) + (full[:WIDTH, 128:] + full[WIDTH:, 128:])


def filter_kernel(index_ref, offset_ref, start_ref, coup_ref, pot_ref, deg_ref, gram_ref, xh_ref, xl_ref, *scratch):
    scratch = iter(scratch)
    field = [[next(scratch) for _ in range(NCH)] for _ in range(3)]
    stack = [[next(scratch) for _ in range(NCH)] for _ in range(3)]
    halo = [[[next(scratch) for _ in range(2)] for _ in range(NCH)] for _ in range(3)]
    partial = next(scratch)
    chosen = [next(scratch) for _ in range(NCH)]
    blocks, row_abs, diag = next(scratch), next(scratch), next(scratch)
    zb, xb, yb = next(scratch), next(scratch), next(scratch)
    degree = next(scratch)
    xt_ref = next(scratch)
    sums = [next(scratch) for _ in range(10)]
    send_sems, recv_sems = next(scratch), next(scratch)
    used = iter(range(COPIES))

    def sems():
        i = next(used)
        return send_sems.at[i], recv_sems.at[i]

    b, st = lax.axis_index("blk"), lax.axis_index("states")
    z, xx, ylo = lax.rem(b, 8), lax.rem(lax.div(b, 8), 4), lax.div(b, 32)
    left, right = (lax.rem(b + 63, 64), st), (lax.rem(b + 1, 64), st)
    z_peers = [(b - z + lax.rem(z + d, 8), st) for d in range(1, 8)]
    x_peers = [(b - xx * 8 + lax.rem(xx + d, 4) * 8, st) for d in range(1, 4)]
    y_peer = (lax.rem(b + 32, 64), st)
    state_peers = [(b, lax.rem(st + d, 4)) for d in range(1, 4)]
    sum_peers = partners()
    peers = [left, right, y_peer] + z_peers + x_peers + state_peers + [peer for group in sum_peers for peer in group]
    barrier = pltpu.get_barrier_semaphore()
    for peer in peers:
        pl.semaphore_signal(barrier, inc=1, device_id=peer, device_id_type=MESH)

    @pl.loop(0, 16)
    def _(s):
        for l in range(2):
            turned = start_ref[l, s].T
            for c in range(NCH):
                part = turned[WIDTH * c : WIDTH * c + WIDTH]
                field[0][c][l, s] = part
                stack[0][c][l, s] = both_halves(part)

    pl.semaphore_wait(barrier, len(peers))
    copies = []
    edge = {}

    def send_edge(k, c, l):
        source = field[k][c].at[l]
        copy = send(source, halo[k][c][1 - l], *sems(), right if l else left)
        copies.append(copy)
        edge[k, c, 1 - l] = copy

    for c in range(NCH):
        send_edge(0, c, 0)
        send_edge(0, c, 1)

    eye = lax.broadcasted_iota(jnp.int32, (128, 128), 0) == lax.broadcasted_iota(jnp.int32, (128, 128), 1)

    @pl.loop(0, 16)
    def _(n):
        turned = coup_ref[n].T
        row_abs[pl.ds(n, 1)] = jnp.sum(jnp.abs(turned), axis=0, keepdims=True)
        diag[pl.ds(n, 1)] = jnp.sum(jnp.where(eye, turned, 0.0), axis=0, keepdims=True)
        blocks[n] = jnp.concatenate(halves(turned), axis=1)

    def bounds_of(s, ends):
        top, low = ends
        for l in range(2):
            first = index_ref[0, l, s]
            middle = diag[pl.ds(first, 1)]
            center = middle + pot_ref[l, pl.ds(s, 1)]
            radius = row_abs[pl.ds(first, 1)] - jnp.abs(middle)
            rest = row_abs[pl.ds(index_ref[1, l, s], 1)]
            for slot in range(2, 7):
                rest = rest + row_abs[pl.ds(index_ref[slot, l, s], 1)]
            radius = radius + rest
            top = jnp.maximum(top, center + radius)
            low = jnp.maximum(low, radius - center)
        return top, low

    least = jnp.full((1, 128), -3e38, F32)
    top, low = lax.fori_loop(0, 16, bounds_of, (least, least))
    zb[z] = jnp.concatenate([jnp.broadcast_to(top, (8, 128)), jnp.broadcast_to(low, (8, 128))], axis=0)

    def exchange(buf, at, group):
        started = [send(buf.at[at], buf.at[at], *sems(), peer) for peer in group]
        copies.extend(started)
        return started

    def merged(buf, started):
        for copy in started:
            copy.wait_recv()
        best = buf[0]
        for i in range(1, buf.shape[0]):
            best = jnp.maximum(best, buf[i])
        return best

    def local_part(k, c):
        @pl.loop(0, 16)
        def _(s):
            for l in range(2):
                sources = [(l, s)]
                for slot in range(1, 5):
                    sources.append((l, (s + offset_ref[slot - 1, l, s]) & 15))
                slots = [0, 1, 2, 3, 4, 6 - l]
                sources.append((1 - l, (s + offset_ref[5 - l, l, s]) & 15))
                lhs = jnp.concatenate([stack[k][c][at] for at in sources], axis=1)
                rhs = jnp.concatenate([blocks[index_ref[slot, l, s]] for slot in slots], axis=0)
                partial[l, s] = product(lhs, rhs)

    def finish(k, c, middle, inverse):
        for l in range(2):
            edge[k, c, l].wait_recv()

            @pl.loop(0, 16)
            def _(s):
                slot = 5 + l
                outer = halo[k][c][l][(s + offset_ref[slot - 1, l, s]) & 15]
                total = partial[l, s] + product(both_halves(outer), blocks[index_ref[slot, l, s]])
                own = field[k][c][l, s]
                new = (total + (pot_ref[l, pl.ds(s, 1)] - middle) * own) * inverse
                if k > 0:
                    new = 2.0 * new - field[k - 1][c][l, s]
                if k < 2:
                    field[k + 1][c][l, s] = new
                    stack[k + 1][c][l, s] = both_halves(new)
                else:
                    d = degree[WIDTH * c : WIDTH * c + WIDTH]
                    chosen[c][s, l] = jnp.where(d == 1, field[1][c][l, s], jnp.where(d == 2, own, new))

            if k < 2:
                send_edge(k + 1, c, l)

    started = exchange(zb, z, z_peers)
    degree[...] = jnp.broadcast_to(deg_ref[...].astype(F32), (128, 128)).T.astype(jnp.int32)
    local_part(0, 0)
    xb[xx] = merged(zb, started)
    started = exchange(xb, xx, x_peers)
    best = merged(xb, started)
    yb[ylo] = best
    started = exchange(yb, ylo, [y_peer])
    best = merged(yb, started)
    upper = jnp.max(best[:8], axis=1, keepdims=True)[:1]
    lower = -jnp.max(best[8:], axis=1, keepdims=True)[:1]
    cut_edge = lower + cut_share * (upper - lower)
    middle = jnp.broadcast_to((upper + cut_edge) / 2.0, (1, 128))
    inverse = jnp.broadcast_to(2.0 / (upper - cut_edge), (1, 128))

    arrivals = []
    for k in range(3):
        for c in range(NCH):
            if (k, c) != (0, 0):
                local_part(k, c)
            finish(k, c, middle, inverse)
            if k == 2:
                rows = pl.ds(pl.multiple_of(128 * st + WIDTH * c, WIDTH), WIDTH)
                for j in range(4) if c == NCH - 1 else [slice(0, 4)]:
                    for d in (1, 2, 3):
                        first = 4 * lax.rem(st + d, 4)
                        part = first + j if c == NCH - 1 else pl.ds(first, 4)
                        copy = send(chosen[c].at[part], xt_ref.at[j, :, rows], *sems(), state_peers[d - 1])
                        copies.append(copy)
                        arrivals.append(copy)
                for s in range(4):
                    for l in range(2):
                        xt_ref[s, l, rows] = chosen[c][4 * st + s, l]
    last = len(arrivals) - 12
    for copy in arrivals[:last]:
        copy.wait_recv()
    packed = sums[0]
    for j in range(4):
        for copy in arrivals[last + 3 * j : last + 3 * j + 3]:
            copy.wait_recv()
        hi, lo = halves(jnp.concatenate([xt_ref[j, 0], xt_ref[j, 1]], axis=1))
        for row in range(4):
            here, upto = slice(128 * row, 128 * row + 128), 128 * row + 128
            block = nt(hi[here], hi[:upto]) + (nt(hi[here], lo[:upto]) + nt(lo[here], hi[:upto]))
            for col in range(row + 1):
                at = slice(128 * SLOT[row, col], 128 * SLOT[row, col] + 128)
                piece = block[:, 128 * col : 128 * col + 128]
                packed[at] = piece if j == 0 else packed[at] + piece

    def meanwhile():
        @pl.loop(0, 8)
        def _(q):
            at = pl.ds(pl.multiple_of(q * 128, 128), 128)
            for d in range(4):
                cols = slice(128 * d, 128 * d + 128)
                xh_ref[at, cols], xl_ref[at, cols] = halves(xt_ref[lax.rem(q, 4), lax.div(q, 4), cols].T)

    sum_everywhere(*sums, gram_ref, sum_peers, sems, copies, meanwhile)
    for copy in copies:
        copy.wait_send()


def partners():
    x, y, z, core = place()
    return (
        [device(lax.rem(x + d, 4), y, z, core) for d in (1, 2, 3)],
        [device(x, lax.rem(y + d, 4), z, core) for d in (1, 2, 3)],
        [device(x, y, lax.rem(z + d, 8), core) for d in range(1, 8)],
        [device(x, y, z, 1 - core)],
    )


def sum_everywhere(packed, r1, a1, ra, rb, a2, b2, ra2, rb2, zbuf, gbuf, peers, sems, copies, meanwhile):
    x, y, z, core = place()
    x_peers, y_peers, z_peers, core_peers = peers

    def spread(group, piece):
        started = [send(*piece(d), *sems(), peer) for d, peer in enumerate(group)]
        copies.extend(started)
        return started

    def arrived(started):
        for copy in started:
            copy.wait_recv()

    def total(own, parts):
        return (own + parts[0]) + (parts[1] + parts[2])

    arrived(spread(core_peers, lambda d: (packed.at[rows_at((1 - core) * 640, 640)], r1)))
    a1[...] = packed[rows_at(core * 640, 640)] + r1[...]
    started = spread(x_peers, lambda d: (a1.at[rows_at(lax.rem(x + d + 1, 4) * 96, 96)], ra.at[d]))
    started += spread(y_peers, lambda d: (a1.at[rows_at(384 + lax.rem(y + d + 1, 4) * 64, 64)], rb.at[d]))
    meanwhile()
    arrived(started)
    a2[...] = total(a1[rows_at(x * 96, 96)], ra)
    b2[...] = total(a1[rows_at(384 + y * 64, 64)], rb)
    started = spread(y_peers, lambda d: (a2.at[rows_at(lax.rem(y + d + 1, 4) * 24, 24)], ra2.at[d]))
    started += spread(x_peers, lambda d: (b2.at[rows_at(lax.rem(x + d + 1, 4) * 16, 16)], rb2.at[d]))
    arrived(started)
    zbuf[z, :24] = total(a2[rows_at(y * 24, 24)], ra2)
    zbuf[z, 24:] = total(b2[rows_at(x * 16, 16)], rb2)
    arrived(spread(z_peers, lambda d: (zbuf.at[z], zbuf.at[z])))
    whole = ((zbuf[0] + zbuf[1]) + (zbuf[2] + zbuf[3])) + ((zbuf[4] + zbuf[5]) + (zbuf[6] + zbuf[7]))
    own_a = rows_at(core * 640 + x * 96 + y * 24, 24)
    own_b = rows_at(core * 640 + 384 + y * 64 + x * 16, 16)
    gbuf[own_a] = whole[:24]
    gbuf[own_b] = whole[24:]
    started = spread(y_peers, lambda d: (gbuf.at[own_a], gbuf.at[own_a]))
    started += spread(x_peers, lambda d: (gbuf.at[own_b], gbuf.at[own_b]))
    arrived(started)
    row_a = rows_at(core * 640 + x * 96, 96)
    row_b = rows_at(core * 640 + 384 + y * 64, 64)
    started = spread(x_peers, lambda d: (gbuf.at[row_a], gbuf.at[row_a]))
    started += spread(y_peers, lambda d: (gbuf.at[row_b], gbuf.at[row_b]))
    arrived(started)
    half = rows_at(core * 640, 640)
    arrived(spread(core_peers, lambda d: (gbuf.at[half], gbuf.at[half])))


def filtered_rows(start_states, couplings, potential, site_offsets, coupling_index, degrees):
    vmem, smem = pl.BlockSpec(memory_space=pltpu.VMEM), pl.BlockSpec(memory_space=pltpu.SMEM)
    scratch = [pltpu.VMEM((2, 16, WIDTH, 128), F32)] * (3 * NCH)
    scratch += [pltpu.VMEM((2, 16, 2 * WIDTH, 128), BF16)] * (3 * NCH)
    scratch += [pltpu.VMEM((16, WIDTH, 128), F32)] * (6 * NCH)
    scratch += [pltpu.VMEM((2, 16, WIDTH, 128), F32)]
    scratch += [pltpu.VMEM((16, 2, WIDTH, 128), F32)] * NCH
    scratch += [pltpu.VMEM((16, 128, 256), BF16), pltpu.VMEM((16, 128), F32), pltpu.VMEM((16, 128), F32)]
    scratch += [pltpu.VMEM((n, 16, 128), F32) for n in (8, 4, 2)]
    scratch += [pltpu.VMEM((128, 128), jnp.int32)]
    scratch += [pltpu.VMEM((4, 2, 512, 128), F32), pltpu.VMEM((1280, 128), F32)]
    scratch += [pltpu.VMEM((640, 128), F32), pltpu.VMEM((640, 128), F32)]
    scratch += [pltpu.VMEM((3, 96, 128), F32), pltpu.VMEM((3, 64, 128), F32)]
    scratch += [pltpu.VMEM((96, 128), F32), pltpu.VMEM((64, 128), F32)]
    scratch += [pltpu.VMEM((3, 24, 128), F32), pltpu.VMEM((3, 16, 128), F32), pltpu.VMEM((8, 40, 128), F32)]
    scratch += [pltpu.SemaphoreType.DMA((COPIES,))] * 2
    return pl.pallas_call(
        filter_kernel,
        out_shape=[
            jax.ShapeDtypeStruct((1280, 128), F32),
            jax.ShapeDtypeStruct((1024, 512), BF16),
            jax.ShapeDtypeStruct((1024, 512), BF16),
        ],
        in_specs=[smem, smem, vmem, vmem, vmem, vmem],
        out_specs=[vmem] * 3,
        scratch_shapes=scratch,
        compiler_params=pltpu.CompilerParams(collective_id=0, has_side_effects=True, vmem_limit_bytes=VMEM_LIMIT),
        name="filter",
    )(coupling_index.transpose(1, 0, 2), site_offsets.transpose(1, 0, 2), start_states, couplings, potential, degrees.reshape(1, 128))


def per_device(start_states, couplings, potential, site_offsets, coupling_index, degrees):
    gram, xh, xl = filtered_rows(start_states, couplings, potential, site_offsets, coupling_index, degrees)
    return orthonormalised(gram, xh, xl).reshape(2, 4, 128, 512)


def solution(mesh):
    in_specs = (
        P("blk", None, None, "states"),
        P(),
        P("blk", None, None),
        P("blk", None, None),
        P("blk", None, None),
        P("states"),
    )
    out_specs = P("blk", "states", None, None)
    return jax.shard_map(
        per_device, mesh=mesh, in_specs=in_specs, out_specs=out_specs, check_vma=False
    )
```

```python
import jax
import jax.numpy as jnp
from jax import lax
from jax.experimental import pallas as pl
from jax.experimental.pallas import tpu as pltpu
from jax.sharding import PartitionSpec as P

cut_share = 0.3

MESH = pl.DeviceIdType.MESH
F32 = jnp.float32
BF16 = jnp.bfloat16
exact = lax.Precision.HIGHEST
VMEM_LIMIT = 60 * 1024 * 1024


def place():
    b, st = lax.axis_index("blk"), lax.axis_index("states")
    z = lax.rem(b, 8)
    x = lax.rem(lax.div(b, 8), 4)
    y = lax.div(st, 2) * 2 + lax.div(b, 32)
    return x, y, z, lax.rem(st, 2)


def device(x, y, z, core):
    return ((lax.rem(y, 2) * 4 + x) * 8 + z, lax.div(y, 2) * 2 + core)


def send(src, dst, send_sem, recv_sem, peer):
    copy = pltpu.make_async_remote_copy(
        src_ref=src, dst_ref=dst, send_sem=send_sem, recv_sem=recv_sem, device_id=peer, device_id_type=MESH
    )
    copy.start()
    return copy


def rows_at(start, size):
    return pl.ds(pl.multiple_of(start, 8), size)


def nt(a, b):
    return lax.dot_general(a, b, (((1,), (1,)), ((), ())), preferred_element_type=F32)


PAIRS = [(i, j) for i in range(4) for j in range(i + 1)]
SLOT = {pair: n for n, pair in enumerate(PAIRS)}


def halves(v):
    hi = v.astype(BF16)
    return hi, (v - hi.astype(F32)).astype(BF16)


def thirds(v):
    hi = v.astype(BF16).astype(F32)
    rest = v - hi
    mid = rest.astype(BF16).astype(F32)
    return hi, mid, rest - mid


def dot_nt(a, b):
    h, m, l = thirds(a)
    u, v, w = thirds(b)
    lhs = jnp.concatenate([h, h, m, m, h, l], axis=1).astype(BF16)
    rhs = jnp.concatenate([u, v, u, v, w, u], axis=1).astype(BF16)
    return lax.dot_general(lhs, rhs, (((1,), (1,)), ((), ())), preferred_element_type=F32)


def dot_nn(a, b):
    h, m, l = thirds(a)
    u, v, w = thirds(b)
    lhs = jnp.concatenate([h, h, m, m, h, l], axis=1).astype(BF16)
    rhs = jnp.concatenate([u, v, u, v, w, u], axis=0).astype(BF16)
    return lax.dot_general(lhs, rhs, (((1,), (0,)), ((), ())), preferred_element_type=F32)


def eliminate(work):
    row = lax.broadcasted_iota(jnp.int32, (16, 128), 0)

    def spread(v, rows=16):
        return jnp.broadcast_to(v, (rows, 128))

    def steps(lo, count):
        left, right = work[lo : lo + 16, :128], work[lo : lo + 16, 128:]
        cols = [spread(left[:, lo + c : lo + c + 1]) for c in range(16)]
        below = []
        for t in range(1, count):
            l2, r2 = work[lo + 16 * t : lo + 16 * t + 16, :128], work[lo + 16 * t : lo + 16 * t + 16, 128:]
            below.append([l2, r2, [spread(l2[:, lo + c : lo + c + 1]) for c in range(16)]])
        for j in range(16):
            scale = lax.rsqrt(jnp.broadcast_to(cols[j][j : j + 1, :], (8, 128)))
            scale = jnp.concatenate([scale] * 2, axis=0)
            factor = jnp.where(row > j, cols[j] * scale, 0.0)
            lrow = spread(left[j : j + 1, :]) * scale
            rrow = spread(right[j : j + 1, :]) * scale
            lower = [part[2][j] * scale for part in below]
            for c in range(j + 1, 16):
                across = spread(cols[c][j : j + 1, :]) * scale
                cols[c] = cols[c] - factor * across
                for part, f in zip(below, lower):
                    part[2][c] = part[2][c] - f * across
            left = jnp.where(row == j, lrow, left - factor * lrow)
            right = jnp.where(row == j, rrow, right - factor * rrow)
            for part, f in zip(below, lower):
                part[0] = part[0] - f * lrow
                part[1] = part[1] - f * rrow
        work[lo : lo + 16, :128] = left
        work[lo : lo + 16, 128:] = right
        for t in range(1, count):
            work[lo + 16 * t : lo + 16 * t + 16, :128] = below[t - 1][0]
            work[lo + 16 * t : lo + 16 * t + 16, 128:] = below[t - 1][1]

    for p in range(128 // PANEL):
        lo = PANEL * p
        for t in range(PANEL // 16):
            steps(lo + 16 * t, PANEL // 16 - t)
        if lo + PANEL < 128:
            h, m, l = thirds(work[lo : lo + PANEL, :])
            lhs = jnp.concatenate([h[:, :128], h[:, :128], m[:, :128], m[:, :128], h[:, :128], l[:, :128]], axis=0).astype(BF16)
            rhs = jnp.concatenate([h, m, h, m, l, h], axis=0).astype(BF16)
            change = lax.dot_general(lhs, rhs, (((0,), (0,)), ((), ())), preferred_element_type=F32)
            work[lo + PANEL :, :] = work[lo + PANEL :, :] - change[lo + PANEL :, :]


PANEL = 32


def factor_kernel(g_ref, xh, xl, out_ref, blocks, work, low, inv, ih, il):
    blocks[...] = g_ref[...]
    inv[...] = jnp.zeros_like(inv)
    eye = (lax.broadcasted_iota(jnp.int32, (128, 128), 0) == lax.broadcasted_iota(jnp.int32, (128, 128), 1)).astype(F32)

    @pl.loop(0, 4)
    def _(k):
        work[:, :128] = blocks[lax.div(k * (k + 1), 2) + k]
        work[:, 128:] = eye
        eliminate(work)
        for n in range(4):

            @pl.when(k == n)
            def _():
                here = slice(128 * n, 128 * n + 128)
                w = work[:, 128:]
                inv[here, here] = w
                if n > 0:
                    known = dot_nn(low[here, : 128 * n], inv[: 128 * n, : 128 * n])
                    inv[here, : 128 * n] = -dot_nn(w, known)
                for i in range(n + 1, 4):
                    low[128 * i : 128 * i + 128, here] = dot_nt(blocks[SLOT[i, n]], w)
                for j in range(n + 1, 4):
                    for i in range(j, 4):
                        blocks[SLOT[i, j]] = blocks[SLOT[i, j]] - dot_nt(
                            low[128 * i : 128 * i + 128, here], low[128 * j : 128 * j + 128, here]
                        )

    ih[...], il[...] = halves(inv[...])

    for i in range(4):
        here, upto = slice(128 * i, 128 * i + 128), 128 * i + 128
        a, b = xh[:, :upto], xl[:, :upto]
        u, v = ih[here, :upto], il[here, :upto]
        out_ref[:, here] = nt(a, u) + (nt(a, v) + nt(b, u))


def orthonormalised(packed, xh, xl):
    vmem = pl.BlockSpec(memory_space=pltpu.VMEM)
    return pl.pallas_call(
        factor_kernel,
        out_shape=jax.ShapeDtypeStruct((1024, 512), F32),
        in_specs=[vmem] * 3,
        out_specs=vmem,
        scratch_shapes=[
            pltpu.VMEM((10, 128, 128), F32),
            pltpu.VMEM((128, 256), F32),
            pltpu.VMEM((512, 512), F32),
            pltpu.VMEM((512, 512), F32),
            pltpu.VMEM((512, 512), BF16),
            pltpu.VMEM((512, 512), BF16),
        ],
        compiler_params=pltpu.CompilerParams(vmem_limit_bytes=VMEM_LIMIT),
        name="factor",
    )(packed.reshape(10, 128, 128), xh, xl)


NCH = 2
WIDTH = 128 // NCH
PARTS = 2
COPIES = 6 * NCH + 2 * (PARTS - 1) + 3 * (NCH + PARTS - 1) + 9 + 11 + 33


def both_halves(v):
    hi, lo = halves(v)
    return jnp.concatenate([hi, lo], axis=0)


def product(lhs, rhs):
    full = lax.dot_general(lhs, rhs, (((1,), (0,)), ((), ())), preferred_element_type=F32)
    half = full.shape[0] // 2
    return (full[:half, :128] + full[half:, :128]) + (full[:half, 128:] + full[half:, 128:])


def parts_of(k, c):
    return PARTS if (k, c) == (2, NCH - 1) else 1


def filter_kernel(index_ref, offset_ref, start_ref, coup_ref, pot_ref, deg_ref, gram_ref, xh_ref, xl_ref, *scratch):
    scratch = iter(scratch)
    field = [[next(scratch) for _ in range(NCH)] for _ in range(3)]
    stack = [[next(scratch) for _ in range(NCH)] for _ in range(3)]
    halo = {}
    for k in range(3):
        for c in range(NCH):
            for part in range(parts_of(k, c)):
                for l in range(2):
                    halo[k, c, l, part] = next(scratch)
    partial = next(scratch)
    chosen = [next(scratch) for _ in range(NCH)]
    blocks, row_abs, diag = next(scratch), next(scratch), next(scratch)
    zb, xb, yb = next(scratch), next(scratch), next(scratch)
    degree = next(scratch)
    xt_ref = next(scratch)
    sums = [next(scratch) for _ in range(10)]
    send_sems, recv_sems = next(scratch), next(scratch)
    used = iter(range(COPIES))

    def sems():
        i = next(used)
        return send_sems.at[i], recv_sems.at[i]

    b, st = lax.axis_index("blk"), lax.axis_index("states")
    z, xx, ylo = lax.rem(b, 8), lax.rem(lax.div(b, 8), 4), lax.div(b, 32)
    left, right = (lax.rem(b + 63, 64), st), (lax.rem(b + 1, 64), st)
    z_peers = [(b - z + lax.rem(z + d, 8), st) for d in range(1, 8)]
    x_peers = [(b - xx * 8 + lax.rem(xx + d, 4) * 8, st) for d in range(1, 4)]
    y_peer = (lax.rem(b + 32, 64), st)
    state_peers = [(b, lax.rem(st + d, 4)) for d in range(1, 4)]
    sum_peers = partners()
    peers = [left, right, y_peer] + z_peers + x_peers + state_peers + [peer for group in sum_peers for peer in group]
    barrier = pltpu.get_barrier_semaphore()
    for peer in peers:
        pl.semaphore_signal(barrier, inc=1, device_id=peer, device_id_type=MESH)

    @pl.loop(0, 16)
    def _(s):
        for l in range(2):
            turned = start_ref[l, s].T
            for c in range(NCH):
                part = turned[WIDTH * c : WIDTH * c + WIDTH]
                field[0][c][l, s] = part
                stack[0][c][l, s] = both_halves(part)

    pl.semaphore_wait(barrier, len(peers))
    copies = []
    edge = {}

    def send_edge(k, c, l):
        size = WIDTH // parts_of(k, c)
        for part in range(parts_of(k, c)):
            source = field[k][c].at[l, :, size * part : size * part + size]
            copy = send(source, halo[k, c, 1 - l, part], *sems(), right if l else left)
            copies.append(copy)
            edge[k, c, 1 - l, part] = copy

    for c in range(NCH):
        send_edge(0, c, 0)
        send_edge(0, c, 1)

    eye = lax.broadcasted_iota(jnp.int32, (128, 128), 0) == lax.broadcasted_iota(jnp.int32, (128, 128), 1)

    @pl.loop(0, 16)
    def _(n):
        turned = coup_ref[n].T
        row_abs[pl.ds(n, 1)] = jnp.sum(jnp.abs(turned), axis=0, keepdims=True)
        diag[pl.ds(n, 1)] = jnp.sum(jnp.where(eye, turned, 0.0), axis=0, keepdims=True)
        blocks[n] = jnp.concatenate(halves(turned), axis=1)

    def bounds_of(s, ends):
        top, low = ends
        for l in range(2):
            first = index_ref[0, l, s]
            middle = diag[pl.ds(first, 1)]
            center = middle + pot_ref[l, pl.ds(s, 1)]
            radius = row_abs[pl.ds(first, 1)] - jnp.abs(middle)
            rest = row_abs[pl.ds(index_ref[1, l, s], 1)]
            for slot in range(2, 7):
                rest = rest + row_abs[pl.ds(index_ref[slot, l, s], 1)]
            radius = radius + rest
            top = jnp.maximum(top, center + radius)
            low = jnp.maximum(low, radius - center)
        return top, low

    least = jnp.full((1, 128), -3e38, F32)
    top, low = lax.fori_loop(0, 16, bounds_of, (least, least))
    zb[z] = jnp.concatenate([jnp.broadcast_to(top, (8, 128)), jnp.broadcast_to(low, (8, 128))], axis=0)

    def exchange(buf, at, group):
        started = [send(buf.at[at], buf.at[at], *sems(), peer) for peer in group]
        copies.extend(started)
        return started

    def merged(buf, started):
        for copy in started:
            copy.wait_recv()
        best = buf[0]
        for i in range(1, buf.shape[0]):
            best = jnp.maximum(best, buf[i])
        return best

    def local_part(k, c):
        @pl.loop(0, 16)
        def _(s):
            for l in range(2):
                sources = [(l, s)]
                for slot in range(1, 5):
                    sources.append((l, (s + offset_ref[slot - 1, l, s]) & 15))
                slots = [0, 1, 2, 3, 4, 6 - l]
                sources.append((1 - l, (s + offset_ref[5 - l, l, s]) & 15))
                lhs = jnp.concatenate([stack[k][c][at] for at in sources], axis=1)
                rhs = jnp.concatenate([blocks[index_ref[slot, l, s]] for slot in slots], axis=0)
                partial[l, s] = product(lhs, rhs)

    def finish(k, c, part, middle, inverse):
        size = WIDTH // parts_of(k, c)
        at = slice(size * part, size * part + size)
        for l in range(2):
            edge[k, c, l, part].wait_recv()

            @pl.loop(0, 16)
            def _(s):
                slot = 5 + l
                outer = halo[k, c, l, part][(s + offset_ref[slot - 1, l, s]) & 15]
                total = partial[l, s, at] + product(both_halves(outer), blocks[index_ref[slot, l, s]])
                own = field[k][c][l, s, at]
                new = (total + (pot_ref[l, pl.ds(s, 1)] - middle) * own) * inverse
                if k > 0:
                    new = 2.0 * new - field[k - 1][c][l, s, at]
                if k < 2:
                    field[k + 1][c][l, s] = new
                    stack[k + 1][c][l, s] = both_halves(new)
                else:
                    d = degree[WIDTH * c + size * part : WIDTH * c + size * part + size]
                    chosen[c][s, l, at] = jnp.where(d == 1, field[1][c][l, s, at], jnp.where(d == 2, own, new))

            if k < 2:
                send_edge(k + 1, c, l)

    started = exchange(zb, z, z_peers)
    degree[...] = jnp.broadcast_to(deg_ref[...].astype(F32), (128, 128)).T.astype(jnp.int32)
    local_part(0, 0)
    xb[xx] = merged(zb, started)
    started = exchange(xb, xx, x_peers)
    best = merged(xb, started)
    yb[ylo] = best
    started = exchange(yb, ylo, [y_peer])
    best = merged(yb, started)
    upper = jnp.max(best[:8], axis=1, keepdims=True)[:1]
    lower = -jnp.max(best[8:], axis=1, keepdims=True)[:1]
    cut_edge = lower + cut_share * (upper - lower)
    middle = jnp.broadcast_to((upper + cut_edge) / 2.0, (1, 128))
    inverse = jnp.broadcast_to(2.0 / (upper - cut_edge), (1, 128))

    arrivals = []
    for k in range(3):
        for c in range(NCH):
            if (k, c) != (0, 0):
                local_part(k, c)
            for part in range(parts_of(k, c)):
                finish(k, c, part, middle, inverse)
                if k < 2:
                    continue
                size = WIDTH // parts_of(k, c)
                at = slice(size * part, size * part + size)
                rows = pl.ds(pl.multiple_of(128 * st + WIDTH * c + size * part, size), size)
                final = c == NCH - 1 and part == PARTS - 1
                for j in range(4) if final else [slice(0, 4)]:
                    for d in (1, 2, 3):
                        first = 4 * lax.rem(st + d, 4)
                        sites = first + j if final else pl.ds(first, 4)
                        source = chosen[c].at[sites, :, at]
                        copy = send(source, xt_ref.at[j, :, rows], *sems(), state_peers[d - 1])
                        copies.append(copy)
                        arrivals.append(copy)
                for s in range(4):
                    for l in range(2):
                        xt_ref[s, l, rows] = chosen[c][4 * st + s, l, at]
    last = len(arrivals) - 12
    for copy in arrivals[:last]:
        copy.wait_recv()
    packed = sums[0]
    for j in range(4):
        for copy in arrivals[last + 3 * j : last + 3 * j + 3]:
            copy.wait_recv()
        hi, lo = halves(jnp.concatenate([xt_ref[j, 0], xt_ref[j, 1]], axis=1))
        for row in range(4):
            here, upto = slice(128 * row, 128 * row + 128), 128 * row + 128
            block = nt(hi[here], hi[:upto]) + (nt(hi[here], lo[:upto]) + nt(lo[here], hi[:upto]))
            for col in range(row + 1):
                at = slice(128 * SLOT[row, col], 128 * SLOT[row, col] + 128)
                piece = block[:, 128 * col : 128 * col + 128]
                packed[at] = piece if j == 0 else packed[at] + piece

    def meanwhile():
        @pl.loop(0, 8)
        def _(q):
            at = pl.ds(pl.multiple_of(q * 128, 128), 128)
            for d in range(4):
                cols = slice(128 * d, 128 * d + 128)
                xh_ref[at, cols], xl_ref[at, cols] = halves(xt_ref[lax.rem(q, 4), lax.div(q, 4), cols].T)

    sum_everywhere(*sums, gram_ref, sum_peers, sems, copies, meanwhile)
    for copy in copies:
        copy.wait_send()


def partners():
    x, y, z, core = place()
    return (
        [device(lax.rem(x + d, 4), y, z, core) for d in (1, 2, 3)],
        [device(x, lax.rem(y + d, 4), z, core) for d in (1, 2, 3)],
        [device(x, y, lax.rem(z + d, 8), core) for d in range(1, 8)],
        [device(x, y, z, 1 - core)],
    )


def sum_everywhere(packed, r1, a1, ra, rb, a2, b2, ra2, rb2, zbuf, gbuf, peers, sems, copies, meanwhile):
    x, y, z, core = place()
    x_peers, y_peers, z_peers, core_peers = peers

    def spread(group, piece):
        started = [send(*piece(d), *sems(), peer) for d, peer in enumerate(group)]
        copies.extend(started)
        return started

    def arrived(started):
        for copy in started:
            copy.wait_recv()

    def total(own, parts):
        return (own + parts[0]) + (parts[1] + parts[2])

    arrived(spread(core_peers, lambda d: (packed.at[rows_at((1 - core) * 640, 640)], r1)))
    a1[...] = packed[rows_at(core * 640, 640)] + r1[...]
    started = spread(x_peers, lambda d: (a1.at[rows_at(lax.rem(x + d + 1, 4) * 96, 96)], ra.at[d]))
    started += spread(y_peers, lambda d: (a1.at[rows_at(384 + lax.rem(y + d + 1, 4) * 64, 64)], rb.at[d]))
    meanwhile()
    arrived(started)
    a2[...] = total(a1[rows_at(x * 96, 96)], ra)
    b2[...] = total(a1[rows_at(384 + y * 64, 64)], rb)
    started = spread(y_peers, lambda d: (a2.at[rows_at(lax.rem(y + d + 1, 4) * 24, 24)], ra2.at[d]))
    started += spread(x_peers, lambda d: (b2.at[rows_at(lax.rem(x + d + 1, 4) * 16, 16)], rb2.at[d]))
    arrived(started)
    zbuf[z, :24] = total(a2[rows_at(y * 24, 24)], ra2)
    zbuf[z, 24:] = total(b2[rows_at(x * 16, 16)], rb2)
    arrived(spread(z_peers, lambda d: (zbuf.at[z], zbuf.at[z])))
    whole = ((zbuf[0] + zbuf[1]) + (zbuf[2] + zbuf[3])) + ((zbuf[4] + zbuf[5]) + (zbuf[6] + zbuf[7]))
    own_a = rows_at(core * 640 + x * 96 + y * 24, 24)
    own_b = rows_at(core * 640 + 384 + y * 64 + x * 16, 16)
    gbuf[own_a] = whole[:24]
    gbuf[own_b] = whole[24:]
    started = spread(y_peers, lambda d: (gbuf.at[own_a], gbuf.at[own_a]))
    started += spread(x_peers, lambda d: (gbuf.at[own_b], gbuf.at[own_b]))
    arrived(started)
    row_a = rows_at(core * 640 + x * 96, 96)
    row_b = rows_at(core * 640 + 384 + y * 64, 64)
    started = spread(x_peers, lambda d: (gbuf.at[row_a], gbuf.at[row_a]))
    started += spread(y_peers, lambda d: (gbuf.at[row_b], gbuf.at[row_b]))
    arrived(started)
    half = rows_at(core * 640, 640)
    arrived(spread(core_peers, lambda d: (gbuf.at[half], gbuf.at[half])))


def filtered_rows(start_states, couplings, potential, site_offsets, coupling_index, degrees):
    vmem, smem = pl.BlockSpec(memory_space=pltpu.VMEM), pl.BlockSpec(memory_space=pltpu.SMEM)
    scratch = [pltpu.VMEM((2, 16, WIDTH, 128), F32)] * (3 * NCH)
    scratch += [pltpu.VMEM((2, 16, 2 * WIDTH, 128), BF16)] * (3 * NCH)
    for k in range(3):
        for c in range(NCH):
            scratch += [pltpu.VMEM((16, WIDTH // parts_of(k, c), 128), F32)] * (2 * parts_of(k, c))
    scratch += [pltpu.VMEM((2, 16, WIDTH, 128), F32)]
    scratch += [pltpu.VMEM((16, 2, WIDTH, 128), F32)] * NCH
    scratch += [pltpu.VMEM((16, 128, 256), BF16), pltpu.VMEM((16, 128), F32), pltpu.VMEM((16, 128), F32)]
    scratch += [pltpu.VMEM((n, 16, 128), F32) for n in (8, 4, 2)]
    scratch += [pltpu.VMEM((128, 128), jnp.int32)]
    scratch += [pltpu.VMEM((4, 2, 512, 128), F32), pltpu.VMEM((1280, 128), F32)]
    scratch += [pltpu.VMEM((640, 128), F32), pltpu.VMEM((640, 128), F32)]
    scratch += [pltpu.VMEM((3, 96, 128), F32), pltpu.VMEM((3, 64, 128), F32)]
    scratch += [pltpu.VMEM((96, 128), F32), pltpu.VMEM((64, 128), F32)]
    scratch += [pltpu.VMEM((3, 24, 128), F32), pltpu.VMEM((3, 16, 128), F32), pltpu.VMEM((8, 40, 128), F32)]
    scratch += [pltpu.SemaphoreType.DMA((COPIES,))] * 2
    return pl.pallas_call(
        filter_kernel,
        out_shape=[
            jax.ShapeDtypeStruct((1280, 128), F32),
            jax.ShapeDtypeStruct((1024, 512), BF16),
            jax.ShapeDtypeStruct((1024, 512), BF16),
        ],
        in_specs=[smem, smem, vmem, vmem, vmem, vmem],
        out_specs=[vmem] * 3,
        scratch_shapes=scratch,
        compiler_params=pltpu.CompilerParams(collective_id=0, has_side_effects=True, vmem_limit_bytes=VMEM_LIMIT),
        name="filter",
    )(coupling_index.transpose(1, 0, 2), site_offsets.transpose(1, 0, 2), start_states, couplings, potential, degrees.reshape(1, 128))


def per_device(start_states, couplings, potential, site_offsets, coupling_index, degrees):
    gram, xh, xl = filtered_rows(start_states, couplings, potential, site_offsets, coupling_index, degrees)
    return orthonormalised(gram, xh, xl).reshape(2, 4, 128, 512)


def solution(mesh):
    in_specs = (
        P("blk", None, None, "states"),
        P(),
        P("blk", None, None),
        P("blk", None, None),
        P("blk", None, None),
        P("states"),
    )
    out_specs = P("blk", "states", None, None)
    return jax.shard_map(
        per_device, mesh=mesh, in_specs=in_specs, out_specs=out_specs, check_vma=False
    )
```

```python
import jax
import jax.numpy as jnp
from jax import lax
from jax.experimental import pallas as pl
from jax.experimental.pallas import tpu as pltpu
from jax.sharding import PartitionSpec as P

cut_share = 0.3

MESH = pl.DeviceIdType.MESH
F32 = jnp.float32
BF16 = jnp.bfloat16
exact = lax.Precision.HIGHEST
VMEM_LIMIT = 60 * 1024 * 1024


def place():
    b, st = lax.axis_index("blk"), lax.axis_index("states")
    z = lax.rem(b, 8)
    x = lax.rem(lax.div(b, 8), 4)
    y = lax.div(st, 2) * 2 + lax.div(b, 32)
    return x, y, z, lax.rem(st, 2)


def device(x, y, z, core):
    return ((lax.rem(y, 2) * 4 + x) * 8 + z, lax.div(y, 2) * 2 + core)


def send(src, dst, send_sem, recv_sem, peer):
    copy = pltpu.make_async_remote_copy(
        src_ref=src, dst_ref=dst, send_sem=send_sem, recv_sem=recv_sem, device_id=peer, device_id_type=MESH
    )
    copy.start()
    return copy


def rows_at(start, size):
    return pl.ds(pl.multiple_of(start, 8), size)


def nt(a, b):
    return lax.dot_general(a, b, (((1,), (1,)), ((), ())), preferred_element_type=F32)


PAIRS = [(i, j) for i in range(4) for j in range(i + 1)]
SLOT = {pair: n for n, pair in enumerate(PAIRS)}


def halves(v):
    hi = v.astype(BF16)
    return hi, (v - hi.astype(F32)).astype(BF16)


def thirds(v):
    hi = v.astype(BF16).astype(F32)
    rest = v - hi
    mid = rest.astype(BF16).astype(F32)
    return hi, mid, rest - mid


def dot_nt(a, b):
    h, m, l = thirds(a)
    u, v, w = thirds(b)
    lhs = jnp.concatenate([h, h, m, m, h, l], axis=1).astype(BF16)
    rhs = jnp.concatenate([u, v, u, v, w, u], axis=1).astype(BF16)
    return lax.dot_general(lhs, rhs, (((1,), (1,)), ((), ())), preferred_element_type=F32)


def dot_nn(a, b):
    h, m, l = thirds(a)
    u, v, w = thirds(b)
    lhs = jnp.concatenate([h, h, m, m, h, l], axis=1).astype(BF16)
    rhs = jnp.concatenate([u, v, u, v, w, u], axis=0).astype(BF16)
    return lax.dot_general(lhs, rhs, (((1,), (0,)), ((), ())), preferred_element_type=F32)


def eliminate(work):
    row = lax.broadcasted_iota(jnp.int32, (16, 128), 0)

    def spread(v, rows=16):
        return jnp.broadcast_to(v, (rows, 128))

    def steps(lo, count):
        left, right = work[lo : lo + 16, :128], work[lo : lo + 16, 128:]
        cols = [spread(left[:, lo + c : lo + c + 1]) for c in range(16)]
        below = []
        for t in range(1, count):
            l2, r2 = work[lo + 16 * t : lo + 16 * t + 16, :128], work[lo + 16 * t : lo + 16 * t + 16, 128:]
            below.append([l2, r2, [spread(l2[:, lo + c : lo + c + 1]) for c in range(16)]])
        for j in range(16):
            scale = lax.rsqrt(jnp.broadcast_to(cols[j][j : j + 1, :], (8, 128)))
            scale = jnp.concatenate([scale] * 2, axis=0)
            factor = jnp.where(row > j, cols[j] * scale, 0.0)
            lrow = spread(left[j : j + 1, :]) * scale
            rrow = spread(right[j : j + 1, :]) * scale
            lower = [part[2][j] * scale for part in below]
            for c in range(j + 1, 16):
                across = spread(cols[c][j : j + 1, :]) * scale
                cols[c] = cols[c] - factor * across
                for part, f in zip(below, lower):
                    part[2][c] = part[2][c] - f * across
            left = jnp.where(row == j, lrow, left - factor * lrow)
            right = jnp.where(row == j, rrow, right - factor * rrow)
            for part, f in zip(below, lower):
                part[0] = part[0] - f * lrow
                part[1] = part[1] - f * rrow
        work[lo : lo + 16, :128] = left
        work[lo : lo + 16, 128:] = right
        for t in range(1, count):
            work[lo + 16 * t : lo + 16 * t + 16, :128] = below[t - 1][0]
            work[lo + 16 * t : lo + 16 * t + 16, 128:] = below[t - 1][1]

    for p in range(128 // PANEL):
        lo = PANEL * p
        for t in range(PANEL // 16):
            steps(lo + 16 * t, PANEL // 16 - t)
        if lo + PANEL < 128:
            h, m, l = thirds(work[lo : lo + PANEL, :])
            lhs = jnp.concatenate([h[:, :128], h[:, :128], m[:, :128], m[:, :128], h[:, :128], l[:, :128]], axis=0).astype(BF16)
            rhs = jnp.concatenate([h, m, h, m, l, h], axis=0).astype(BF16)
            change = lax.dot_general(lhs, rhs, (((0,), (0,)), ((), ())), preferred_element_type=F32)
            work[lo + PANEL :, :] = work[lo + PANEL :, :] - change[lo + PANEL :, :]


PANEL = 32


def factor_kernel(g_ref, xh, xl, out_ref, blocks, work, low, inv, ih, il):
    blocks[...] = g_ref[...]
    inv[...] = jnp.zeros_like(inv)
    eye = (lax.broadcasted_iota(jnp.int32, (128, 128), 0) == lax.broadcasted_iota(jnp.int32, (128, 128), 1)).astype(F32)

    @pl.loop(0, 4)
    def _(k):
        work[:, :128] = blocks[lax.div(k * (k + 1), 2) + k]
        work[:, 128:] = eye
        eliminate(work)
        for n in range(4):

            @pl.when(k == n)
            def _():
                here = slice(128 * n, 128 * n + 128)
                w = work[:, 128:]
                inv[here, here] = w
                if n > 0:
                    known = dot_nn(low[here, : 128 * n], inv[: 128 * n, : 128 * n])
                    inv[here, : 128 * n] = -dot_nn(w, known)
                for i in range(n + 1, 4):
                    low[128 * i : 128 * i + 128, here] = dot_nt(blocks[SLOT[i, n]], w)
                for j in range(n + 1, 4):
                    for i in range(j, 4):
                        blocks[SLOT[i, j]] = blocks[SLOT[i, j]] - dot_nt(
                            low[128 * i : 128 * i + 128, here], low[128 * j : 128 * j + 128, here]
                        )

    ih[...], il[...] = halves(inv[...])

    for i in range(4):
        here, upto = slice(128 * i, 128 * i + 128), 128 * i + 128
        a, b = xh[:, :upto], xl[:, :upto]
        u, v = ih[here, :upto], il[here, :upto]
        out_ref[:, here] = nt(a, u) + (nt(a, v) + nt(b, u))


def orthonormalised(packed, xh, xl):
    vmem = pl.BlockSpec(memory_space=pltpu.VMEM)
    return pl.pallas_call(
        factor_kernel,
        out_shape=jax.ShapeDtypeStruct((1024, 512), F32),
        in_specs=[vmem] * 3,
        out_specs=vmem,
        scratch_shapes=[
            pltpu.VMEM((10, 128, 128), F32),
            pltpu.VMEM((128, 256), F32),
            pltpu.VMEM((512, 512), F32),
            pltpu.VMEM((512, 512), F32),
            pltpu.VMEM((512, 512), BF16),
            pltpu.VMEM((512, 512), BF16),
        ],
        compiler_params=pltpu.CompilerParams(vmem_limit_bytes=VMEM_LIMIT),
        name="factor",
    )(packed.reshape(10, 128, 128), xh, xl)


NCH = 2
WIDTH = 128 // NCH
PARTS = 1
AHEAD = 1
ORDER = [(k, c) for k in range(3) for c in range(NCH)]
COPIES = 6 * NCH + 2 * (PARTS - 1) + 3 * (NCH + PARTS - 1) + 9 + 11 + 47


def both_halves(v):
    hi, lo = halves(v)
    return jnp.concatenate([hi, lo], axis=0)


def product(lhs, rhs):
    full = lax.dot_general(lhs, rhs, (((1,), (0,)), ((), ())), preferred_element_type=F32)
    half = full.shape[0] // 2
    return (full[:half, :128] + full[half:, :128]) + (full[:half, 128:] + full[half:, 128:])


def parts_of(k, c):
    return PARTS if (k, c) == (2, NCH - 1) else 1


def filter_kernel(index_ref, offset_ref, start_ref, coup_ref, pot_ref, deg_ref, gram_ref, xh_ref, xl_ref, *scratch):
    scratch = iter(scratch)
    field = [[next(scratch) for _ in range(NCH)] for _ in range(3)]
    stack = [[next(scratch) for _ in range(NCH)] for _ in range(3)]
    halo = {}
    for k in range(3):
        for c in range(NCH):
            for part in range(parts_of(k, c)):
                for l in range(2):
                    halo[k, c, l, part] = next(scratch)
    partial = next(scratch)
    chosen = [next(scratch) for _ in range(NCH)]
    blocks, row_abs, diag = next(scratch), next(scratch), next(scratch)
    zb, xb, yb = next(scratch), next(scratch), next(scratch)
    degree = next(scratch)
    xt_ref = next(scratch)
    sums = [next(scratch) for _ in range(10)]
    send_sems, recv_sems = next(scratch), next(scratch)
    used = iter(range(COPIES))

    def sems():
        i = next(used)
        return send_sems.at[i], recv_sems.at[i]

    b, st = lax.axis_index("blk"), lax.axis_index("states")
    z, xx, ylo = lax.rem(b, 8), lax.rem(lax.div(b, 8), 4), lax.div(b, 32)
    left, right = (lax.rem(b + 63, 64), st), (lax.rem(b + 1, 64), st)
    z_peers = [(b - z + lax.rem(z + d, 8), st) for d in range(1, 8)]
    x_peers = [(b - xx * 8 + lax.rem(xx + d, 4) * 8, st) for d in range(1, 4)]
    y_peer = (lax.rem(b + 32, 64), st)
    state_peers = [(b, lax.rem(st + d, 4)) for d in range(1, 4)]
    sum_peers = partners()
    peers = [left, right, y_peer] + z_peers + x_peers + state_peers + [peer for group in sum_peers for peer in group]
    barrier = pltpu.get_barrier_semaphore()
    for peer in peers:
        pl.semaphore_signal(barrier, inc=1, device_id=peer, device_id_type=MESH)

    @pl.loop(0, 16, unroll=2)
    def _(s):
        for l in range(2):
            turned = start_ref[l, s].T
            for c in range(NCH):
                part = turned[WIDTH * c : WIDTH * c + WIDTH]
                field[0][c][l, s] = part
                stack[0][c][l, s] = both_halves(part)

    pl.semaphore_wait(barrier, len(peers))
    copies = []
    edge = {}

    def send_edge(k, c, l):
        size = WIDTH // parts_of(k, c)
        for part in range(parts_of(k, c)):
            source = field[k][c].at[l, :, size * part : size * part + size]
            copy = send(source, halo[k, c, 1 - l, part], *sems(), right if l else left)
            if ORDER.index((k, c)) + AHEAD >= len(ORDER):
                copies.append(copy)
            edge[k, c, 1 - l, part] = copy

    for n in range(AHEAD):
        send_edge(*ORDER[n], 0)
        send_edge(*ORDER[n], 1)

    eye = lax.broadcasted_iota(jnp.int32, (128, 128), 0) == lax.broadcasted_iota(jnp.int32, (128, 128), 1)

    @pl.loop(0, 16, unroll=2)
    def _(n):
        turned = coup_ref[n].T
        row_abs[pl.ds(n, 1)] = jnp.sum(jnp.abs(turned), axis=0, keepdims=True)
        diag[pl.ds(n, 1)] = jnp.sum(jnp.where(eye, turned, 0.0), axis=0, keepdims=True)
        blocks[n] = jnp.concatenate(halves(turned), axis=1)

    def bounds_of(s, ends):
        top, low = ends
        for l in range(2):
            first = index_ref[0, l, s]
            middle = diag[pl.ds(first, 1)]
            center = middle + pot_ref[l, pl.ds(s, 1)]
            radius = row_abs[pl.ds(first, 1)] - jnp.abs(middle)
            rest = row_abs[pl.ds(index_ref[1, l, s], 1)]
            for slot in range(2, 7):
                rest = rest + row_abs[pl.ds(index_ref[slot, l, s], 1)]
            radius = radius + rest
            top = jnp.maximum(top, center + radius)
            low = jnp.maximum(low, radius - center)
        return top, low

    least = jnp.full((1, 128), -3e38, F32)
    top, low = lax.fori_loop(0, 16, bounds_of, (least, least))
    zb[z] = jnp.concatenate([jnp.broadcast_to(top, (8, 128)), jnp.broadcast_to(low, (8, 128))], axis=0)

    def exchange(buf, at, group):
        started = [send(buf.at[at], buf.at[at], *sems(), peer) for peer in group]
        copies.extend(started)
        return started

    def merged(buf, started):
        for copy in started:
            copy.wait_recv()
        best = buf[0]
        for i in range(1, buf.shape[0]):
            best = jnp.maximum(best, buf[i])
        return best

    def local_part(k, c):
        @pl.loop(0, 16, unroll=4)
        def _(s):
            for l in range(2):
                sources = [(l, s)]
                for slot in range(1, 5):
                    sources.append((l, (s + offset_ref[slot - 1, l, s]) & 15))
                slots = [0, 1, 2, 3, 4, 6 - l]
                sources.append((1 - l, (s + offset_ref[5 - l, l, s]) & 15))
                lhs = jnp.concatenate([stack[k][c][at] for at in sources], axis=1)
                rhs = jnp.concatenate([blocks[index_ref[slot, l, s]] for slot in slots], axis=0)
                partial[l, s] = product(lhs, rhs)

    def finish(k, c, part, middle, inverse):
        size = WIDTH // parts_of(k, c)
        at = slice(size * part, size * part + size)
        for l in range(2):
            edge[k, c, l, part].wait_recv()

            @pl.loop(0, 16, unroll=8)
            def _(s):
                slot = 5 + l
                outer = halo[k, c, l, part][(s + offset_ref[slot - 1, l, s]) & 15]
                total = partial[l, s, at] + product(both_halves(outer), blocks[index_ref[slot, l, s]])
                own = field[k][c][l, s, at]
                new = (total + (pot_ref[l, pl.ds(s, 1)] - middle) * own) * inverse
                if k > 0:
                    new = 2.0 * new - field[k - 1][c][l, s, at]
                if k < 2:
                    field[k + 1][c][l, s] = new
                    stack[k + 1][c][l, s] = both_halves(new)
                else:
                    d = degree[WIDTH * c + size * part : WIDTH * c + size * part + size]
                    chosen[c][s, l, at] = jnp.where(d == 1, field[1][c][l, s, at], jnp.where(d == 2, own, new))

    started = exchange(zb, z, z_peers)
    degree[...] = jnp.broadcast_to(deg_ref[...].astype(F32), (128, 128)).T.astype(jnp.int32)
    local_part(0, 0)
    xb[xx] = merged(zb, started)
    started = exchange(xb, xx, x_peers)
    best = merged(xb, started)
    yb[ylo] = best
    started = exchange(yb, ylo, [y_peer])
    best = merged(yb, started)
    upper = jnp.max(best[:8], axis=1, keepdims=True)[:1]
    lower = -jnp.max(best[8:], axis=1, keepdims=True)[:1]
    cut_edge = lower + cut_share * (upper - lower)
    middle = jnp.broadcast_to((upper + cut_edge) / 2.0, (1, 128))
    inverse = jnp.broadcast_to(2.0 / (upper - cut_edge), (1, 128))

    arrivals = []

    def send_next(n):
        if n + AHEAD < len(ORDER):
            for l in range(2):
                edge[*ORDER[n], 1 - l, 0].wait_send()
                send_edge(*ORDER[n + AHEAD], l)

    def hand_out(c):
        rows = pl.ds(pl.multiple_of(128 * st + WIDTH * c, WIDTH), WIDTH)
        final = c == NCH - 1
        for j in range(4) if final else [slice(0, 4)]:
            for d in (1, 2, 3):
                first = 4 * lax.rem(st + d, 4)
                source = chosen[c].at[first + j if final else pl.ds(first, 4)]
                copy = send(source, xt_ref.at[j, :, rows], *sems(), state_peers[d - 1])
                copies.append(copy)
                arrivals.append(copy)
        for s in range(4):
            for l in range(2):
                xt_ref[s, l, rows] = chosen[c][4 * st + s, l]

    send_next(0)
    for n, (k, c) in enumerate(ORDER):
        finish(k, c, 0, middle, inverse)
        if k == 2:
            hand_out(c)
        if n + 1 < len(ORDER):
            local_part(*ORDER[n + 1])
            send_next(n + 1)
    last = len(arrivals) - 12
    for copy in arrivals[:last]:
        copy.wait_recv()
    packed = sums[0]
    for j in range(4):
        for copy in arrivals[last + 3 * j : last + 3 * j + 3]:
            copy.wait_recv()
        hi, lo = halves(jnp.concatenate([xt_ref[j, 0], xt_ref[j, 1]], axis=1))
        for row in range(4):
            here, upto = slice(128 * row, 128 * row + 128), 128 * row + 128
            block = nt(hi[here], hi[:upto]) + (nt(hi[here], lo[:upto]) + nt(lo[here], hi[:upto]))
            for col in range(row + 1):
                at = slice(128 * SLOT[row, col], 128 * SLOT[row, col] + 128)
                piece = block[:, 128 * col : 128 * col + 128]
                packed[at] = piece if j == 0 else packed[at] + piece

    def meanwhile():
        @pl.loop(0, 8)
        def _(q):
            at = pl.ds(pl.multiple_of(q * 128, 128), 128)
            for d in range(4):
                cols = slice(128 * d, 128 * d + 128)
                xh_ref[at, cols], xl_ref[at, cols] = halves(xt_ref[lax.rem(q, 4), lax.div(q, 4), cols].T)

    sum_everywhere(*sums, gram_ref, sum_peers, sems, copies, meanwhile)
    for copy in copies:
        copy.wait_send()


def partners():
    x, y, z, core = place()
    return (
        [device(lax.rem(x + d, 4), y, z, core) for d in (1, 2, 3)],
        [device(x, lax.rem(y + d, 4), z, core) for d in (1, 2, 3)],
        [device(x, y, lax.rem(z + d, 8), core) for d in range(1, 8)],
        [device(x, y, z, 1 - core)],
    )


def sum_everywhere(packed, r1, a1, ra, rb, a2, b2, ra2, rb2, zbuf, gbuf, peers, sems, copies, meanwhile):
    x, y, z, core = place()
    x_peers, y_peers, z_peers, core_peers = peers

    def spread(group, piece):
        started = [send(*piece(d), *sems(), peer) for d, peer in enumerate(group)]
        copies.extend(started)
        return started

    def arrived(started):
        for copy in started:
            copy.wait_recv()

    def total(own, parts):
        return (own + parts[0]) + (parts[1] + parts[2])

    def one(source, target, peer):
        copies.append(send(source, target, *sems(), peer))
        return copies[-1]

    def piece_a(d):
        return lax.rem(x + d, 4) * 96

    def piece_b(d):
        return 384 + lax.rem(y + d, 4) * 64

    pieces = [(piece_a(d), 96, x_peers, ra, d) for d in (1, 2, 3, 0)], [(piece_b(d), 64, y_peers, rb, d) for d in (1, 2, 3, 0)]
    pieces = [piece for pair in zip(*pieces) for piece in pair]
    landing = [
        one(packed.at[rows_at((1 - core) * 640 + at, size)], r1.at[rows_at(at, size)], core_peers[0])
        for at, size, _, _, _ in pieces
    ]
    started = []
    for copy, (at, size, group, target, d) in zip(landing, pieces):
        copy.wait_recv()
        a1[rows_at(at, size)] = packed[rows_at(core * 640 + at, size)] + r1[rows_at(at, size)]
        if d > 0:
            started.append(one(a1.at[rows_at(at, size)], target.at[d - 1], group[d - 1]))
    meanwhile()
    arrived(started)
    a2[...] = total(a1[rows_at(x * 96, 96)], ra)
    b2[...] = total(a1[rows_at(384 + y * 64, 64)], rb)
    started = spread(y_peers, lambda d: (a2.at[rows_at(lax.rem(y + d + 1, 4) * 24, 24)], ra2.at[d]))
    started += spread(x_peers, lambda d: (b2.at[rows_at(lax.rem(x + d + 1, 4) * 16, 16)], rb2.at[d]))
    arrived(started)
    zbuf[z, :24] = total(a2[rows_at(y * 24, 24)], ra2)
    zbuf[z, 24:] = total(b2[rows_at(x * 16, 16)], rb2)
    arrived(spread(z_peers, lambda d: (zbuf.at[z], zbuf.at[z])))
    whole = ((zbuf[0] + zbuf[1]) + (zbuf[2] + zbuf[3])) + ((zbuf[4] + zbuf[5]) + (zbuf[6] + zbuf[7]))
    own_a = rows_at(core * 640 + x * 96 + y * 24, 24)
    own_b = rows_at(core * 640 + 384 + y * 64 + x * 16, 16)
    gbuf[own_a] = whole[:24]
    gbuf[own_b] = whole[24:]
    started = spread(y_peers, lambda d: (gbuf.at[own_a], gbuf.at[own_a]))
    started += spread(x_peers, lambda d: (gbuf.at[own_b], gbuf.at[own_b]))
    arrived(started)

    def share(at, size, peer):
        rows = rows_at(core * 640 + at, size)
        return one(gbuf.at[rows], gbuf.at[rows], peer)

    started = []
    for d in range(3):
        started.append((share(x * 96, 96, x_peers[d]), piece_a(3 - d), 96))
        started.append((share(384 + y * 64, 64, y_peers[d]), piece_b(3 - d), 64))
    landing = [share(x * 96, 96, core_peers[0]), share(384 + y * 64, 64, core_peers[0])]
    for copy, at, size in started:
        copy.wait_recv()
        landing.append(share(at, size, core_peers[0]))
    arrived(landing)


def filtered_rows(start_states, couplings, potential, site_offsets, coupling_index, degrees):
    vmem, smem = pl.BlockSpec(memory_space=pltpu.VMEM), pl.BlockSpec(memory_space=pltpu.SMEM)
    scratch = [pltpu.VMEM((2, 16, WIDTH, 128), F32)] * (3 * NCH)
    scratch += [pltpu.VMEM((2, 16, 2 * WIDTH, 128), BF16)] * (3 * NCH)
    for k in range(3):
        for c in range(NCH):
            scratch += [pltpu.VMEM((16, WIDTH // parts_of(k, c), 128), F32)] * (2 * parts_of(k, c))
    scratch += [pltpu.VMEM((2, 16, WIDTH, 128), F32)]
    scratch += [pltpu.VMEM((16, 2, WIDTH, 128), F32)] * NCH
    scratch += [pltpu.VMEM((16, 128, 256), BF16), pltpu.VMEM((16, 128), F32), pltpu.VMEM((16, 128), F32)]
    scratch += [pltpu.VMEM((n, 16, 128), F32) for n in (8, 4, 2)]
    scratch += [pltpu.VMEM((128, 128), jnp.int32)]
    scratch += [pltpu.VMEM((4, 2, 512, 128), F32), pltpu.VMEM((1280, 128), F32)]
    scratch += [pltpu.VMEM((640, 128), F32), pltpu.VMEM((640, 128), F32)]
    scratch += [pltpu.VMEM((3, 96, 128), F32), pltpu.VMEM((3, 64, 128), F32)]
    scratch += [pltpu.VMEM((96, 128), F32), pltpu.VMEM((64, 128), F32)]
    scratch += [pltpu.VMEM((3, 24, 128), F32), pltpu.VMEM((3, 16, 128), F32), pltpu.VMEM((8, 40, 128), F32)]
    scratch += [pltpu.SemaphoreType.DMA((COPIES,))] * 2
    return pl.pallas_call(
        filter_kernel,
        out_shape=[
            jax.ShapeDtypeStruct((1280, 128), F32),
            jax.ShapeDtypeStruct((1024, 512), BF16),
            jax.ShapeDtypeStruct((1024, 512), BF16),
        ],
        in_specs=[smem, smem, vmem, vmem, vmem, vmem],
        out_specs=[vmem] * 3,
        scratch_shapes=scratch,
        compiler_params=pltpu.CompilerParams(collective_id=0, has_side_effects=True, vmem_limit_bytes=VMEM_LIMIT),
        name="filter",
    )(coupling_index.transpose(1, 0, 2), site_offsets.transpose(1, 0, 2), start_states, couplings, potential, degrees.reshape(1, 128))


def per_device(start_states, couplings, potential, site_offsets, coupling_index, degrees):
    gram, xh, xl = filtered_rows(start_states, couplings, potential, site_offsets, coupling_index, degrees)
    return orthonormalised(gram, xh, xl).reshape(2, 4, 128, 512)


def solution(mesh):
    in_specs = (
        P("blk", None, None, "states"),
        P(),
        P("blk", None, None),
        P("blk", None, None),
        P("blk", None, None),
        P("states"),
    )
    out_specs = P("blk", "states", None, None)
    return jax.shard_map(
        per_device, mesh=mesh, in_specs=in_specs, out_specs=out_specs, check_vma=False
    )
```

```python
import functools

import jax
import jax.numpy as jnp
from jax import lax
from jax.experimental import pallas as pl
from jax.experimental.pallas import tpu as pltpu
from jax.sharding import PartitionSpec as P

cut_share = 0.3

MESH = pl.DeviceIdType.MESH
F32 = jnp.float32
BF16 = jnp.bfloat16
exact = lax.Precision.HIGHEST
VMEM_LIMIT = 60 * 1024 * 1024


def place():
    b, st = lax.axis_index("blk"), lax.axis_index("states")
    z = lax.rem(b, 8)
    x = lax.rem(lax.div(b, 8), 4)
    y = lax.div(st, 2) * 2 + lax.div(b, 32)
    return x, y, z, lax.rem(st, 2)


def device(x, y, z, core):
    return ((lax.rem(y, 2) * 4 + x) * 8 + z, lax.div(y, 2) * 2 + core)


def send(src, dst, send_sem, recv_sem, peer):
    copy = pltpu.make_async_remote_copy(
        src_ref=src, dst_ref=dst, send_sem=send_sem, recv_sem=recv_sem, device_id=peer, device_id_type=MESH
    )
    copy.start()
    return copy


def rows_at(start, size):
    return pl.ds(pl.multiple_of(start, 8), size)


def nt(a, b):
    return lax.dot_general(a, b, (((1,), (1,)), ((), ())), preferred_element_type=F32)


PAIRS = [(i, j) for i in range(4) for j in range(i + 1)]
SLOT = {pair: n for n, pair in enumerate(PAIRS)}


def halves(v):
    hi = v.astype(BF16)
    return hi, (v - hi.astype(F32)).astype(BF16)


def thirds(v):
    hi = v.astype(BF16).astype(F32)
    rest = v - hi
    mid = rest.astype(BF16).astype(F32)
    return hi, mid, rest - mid


def dot_nt(a, b):
    h, m, l = thirds(a)
    u, v, w = thirds(b)
    lhs = jnp.concatenate([h, h, m, m, h, l], axis=1).astype(BF16)
    rhs = jnp.concatenate([u, v, u, v, w, u], axis=1).astype(BF16)
    return lax.dot_general(lhs, rhs, (((1,), (1,)), ((), ())), preferred_element_type=F32)


def dot_nn(a, b):
    h, m, l = thirds(a)
    u, v, w = thirds(b)
    lhs = jnp.concatenate([h, h, m, m, h, l], axis=1).astype(BF16)
    rhs = jnp.concatenate([u, v, u, v, w, u], axis=0).astype(BF16)
    return lax.dot_general(lhs, rhs, (((1,), (0,)), ((), ())), preferred_element_type=F32)


def eliminate(work, others):
    row = lax.broadcasted_iota(jnp.int32, (16, 128), 0)

    def spread(v, rows=16):
        return jnp.broadcast_to(v, (rows, 128))

    def steps(lo, count):
        left, right = work[lo : lo + 16, :128], work[lo : lo + 16, 128:]
        cols = [spread(left[:, lo + c : lo + c + 1]) for c in range(16)]
        below = []
        for t in range(1, count):
            l2, r2 = work[lo + 16 * t : lo + 16 * t + 16, :128], work[lo + 16 * t : lo + 16 * t + 16, 128:]
            below.append([l2, r2, [spread(l2[:, lo + c : lo + c + 1]) for c in range(16)]])
        for j in range(16):
            scale = lax.rsqrt(jnp.broadcast_to(cols[j][j : j + 1, :], (8, 128)))
            scale = jnp.concatenate([scale] * 2, axis=0)
            factor = jnp.where(row > j, cols[j] * scale, 0.0)
            lrow = spread(left[j : j + 1, :]) * scale
            rrow = spread(right[j : j + 1, :]) * scale
            lower = [part[2][j] * scale for part in below]
            for c in range(j + 1, 16):
                across = spread(cols[c][j : j + 1, :]) * scale
                cols[c] = cols[c] - factor * across
                for part, f in zip(below, lower):
                    part[2][c] = part[2][c] - f * across
            left = jnp.where(row == j, lrow, left - factor * lrow)
            right = jnp.where(row == j, rrow, right - factor * rrow)
            for part, f in zip(below, lower):
                part[0] = part[0] - f * lrow
                part[1] = part[1] - f * rrow
        work[lo : lo + 16, :128] = left
        work[lo : lo + 16, 128:] = right
        for t in range(1, count):
            work[lo + 16 * t : lo + 16 * t + 16, :128] = below[t - 1][0]
            work[lo + 16 * t : lo + 16 * t + 16, 128:] = below[t - 1][1]

    for p in range(128 // PANEL):
        lo = PANEL * p
        for t in range(PANEL // 16):
            steps(lo + 16 * t, PANEL // 16 - t)
            if others:
                others.pop(0)()
        if lo + PANEL < 128:
            h, m, l = thirds(work[lo : lo + PANEL, :])
            lhs = jnp.concatenate([h[:, :128], h[:, :128], m[:, :128], m[:, :128], h[:, :128], l[:, :128]], axis=0).astype(BF16)
            rhs = jnp.concatenate([h, m, h, m, l, h], axis=0).astype(BF16)
            change = lax.dot_general(lhs, rhs, (((0,), (0,)), ((), ())), preferred_element_type=F32)
            work[lo + PANEL :, :] = work[lo + PANEL :, :] - change[lo + PANEL :, :]


PANEL = 32


def factor_kernel(g_ref, xh, xl, out_ref, blocks, work, low, inv):
    blocks[...] = g_ref[...]
    inv[...] = jnp.zeros_like(inv)
    eye = (lax.broadcasted_iota(jnp.int32, (128, 128), 0) == lax.broadcasted_iota(jnp.int32, (128, 128), 1)).astype(F32)

    def lower_block(i, n):
        low[128 * i : 128 * i + 128, 128 * n : 128 * n + 128] = dot_nt(blocks[SLOT[i, n]], work[n, :, 128:])

    def update(i, j, n):
        cols = slice(128 * n, 128 * n + 128)
        blocks[SLOT[i, j]] = blocks[SLOT[i, j]] - dot_nt(
            low[128 * i : 128 * i + 128, cols], low[128 * j : 128 * j + 128, cols]
        )

    def inverse_row(n):
        here = slice(128 * n, 128 * n + 128)
        w = work[n, :, 128:]
        inv[here, here] = w
        if n > 0:
            inv[here, : 128 * n] = -dot_nn(w, dot_nn(low[here, : 128 * n], inv[: 128 * n, : 128 * n]))

    def product_block(n, part):
        here, upto, rows = slice(128 * n, 128 * n + 128), 128 * n + 128, slice(512 * part, 512 * part + 512)
        u, v = halves(inv[here, :upto])
        a, b = xh[rows, :upto], xl[rows, :upto]
        out_ref[rows, here] = nt(a, u) + (nt(a, v) + nt(b, u))

    call = functools.partial
    others = []
    for n in range(4):
        mine = work.at[n]
        mine[:, :128] = blocks[SLOT[n, n]]
        mine[:, 128:] = eye
        eliminate(mine, others)
        while others:
            others.pop(0)()
        if n < 3:
            lower_block(n + 1, n)
            update(n + 1, n + 1, n)
        others = [call(lower_block, i, n) for i in range(n + 2, 4)]
        others += [call(update, i, j, n) for j in range(n + 1, 4) for i in range(max(j, n + 2), 4)]
        others += [call(inverse_row, n), call(product_block, n, 0), call(product_block, n, 1)]
    for other in others:
        other()


def orthonormalised(packed, xh, xl):
    vmem = pl.BlockSpec(memory_space=pltpu.VMEM)
    return pl.pallas_call(
        factor_kernel,
        out_shape=jax.ShapeDtypeStruct((1024, 512), F32),
        in_specs=[vmem] * 3,
        out_specs=vmem,
        scratch_shapes=[
            pltpu.VMEM((10, 128, 128), F32),
            pltpu.VMEM((4, 128, 256), F32),
            pltpu.VMEM((512, 512), F32),
            pltpu.VMEM((512, 512), F32),
        ],
        compiler_params=pltpu.CompilerParams(vmem_limit_bytes=VMEM_LIMIT),
        name="factor",
    )(packed.reshape(10, 128, 128), xh, xl)


NCH = 2
WIDTH = 128 // NCH
PARTS = 1
AHEAD = 1
ORDER = [(k, c) for k in range(3) for c in range(NCH)]
COPIES = 6 * NCH + 2 * (PARTS - 1) + 3 * (NCH + PARTS - 1) + 9 + 11 + 47


def both_halves(v):
    hi, lo = halves(v)
    return jnp.concatenate([hi, lo], axis=0)


def product(lhs, rhs):
    full = lax.dot_general(lhs, rhs, (((1,), (0,)), ((), ())), preferred_element_type=F32)
    half = full.shape[0] // 2
    return (full[:half, :128] + full[half:, :128]) + (full[:half, 128:] + full[half:, 128:])


def parts_of(k, c):
    return PARTS if (k, c) == (2, NCH - 1) else 1


def filter_kernel(index_ref, offset_ref, start_ref, coup_ref, pot_ref, deg_ref, gram_ref, xh_ref, xl_ref, *scratch):
    scratch = iter(scratch)
    field = [[next(scratch) for _ in range(NCH)] for _ in range(3)]
    stack = [[next(scratch) for _ in range(NCH)] for _ in range(3)]
    halo = {}
    for k in range(3):
        for c in range(NCH):
            for part in range(parts_of(k, c)):
                for l in range(2):
                    halo[k, c, l, part] = next(scratch)
    partial = next(scratch)
    chosen = [next(scratch) for _ in range(NCH)]
    blocks, row_abs, diag = next(scratch), next(scratch), next(scratch)
    zb, xb, yb = next(scratch), next(scratch), next(scratch)
    degree = next(scratch)
    xt_ref = next(scratch)
    sums = [next(scratch) for _ in range(10)]
    send_sems, recv_sems = next(scratch), next(scratch)
    used = iter(range(COPIES))

    def sems():
        i = next(used)
        return send_sems.at[i], recv_sems.at[i]

    b, st = lax.axis_index("blk"), lax.axis_index("states")
    z, xx, ylo = lax.rem(b, 8), lax.rem(lax.div(b, 8), 4), lax.div(b, 32)
    left, right = (lax.rem(b + 63, 64), st), (lax.rem(b + 1, 64), st)
    z_peers = [(b - z + lax.rem(z + d, 8), st) for d in range(1, 8)]
    x_peers = [(b - xx * 8 + lax.rem(xx + d, 4) * 8, st) for d in range(1, 4)]
    y_peer = (lax.rem(b + 32, 64), st)
    state_peers = [(b, lax.rem(st + d, 4)) for d in range(1, 4)]
    sum_peers = partners()
    peers = [left, right, y_peer] + z_peers + x_peers + state_peers + [peer for group in sum_peers for peer in group]
    barrier = pltpu.get_barrier_semaphore()
    for peer in peers:
        pl.semaphore_signal(barrier, inc=1, device_id=peer, device_id_type=MESH)

    @pl.loop(0, 16, unroll=2)
    def _(s):
        for l in range(2):
            turned = start_ref[l, s].T
            for c in range(NCH):
                part = turned[WIDTH * c : WIDTH * c + WIDTH]
                field[0][c][l, s] = part
                stack[0][c][l, s] = both_halves(part)

    pl.semaphore_wait(barrier, len(peers))
    copies = []
    edge = {}

    def send_edge(k, c, l):
        size = WIDTH // parts_of(k, c)
        for part in range(parts_of(k, c)):
            source = field[k][c].at[l, :, size * part : size * part + size]
            copy = send(source, halo[k, c, 1 - l, part], *sems(), right if l else left)
            if ORDER.index((k, c)) + AHEAD >= len(ORDER):
                copies.append(copy)
            edge[k, c, 1 - l, part] = copy

    for n in range(AHEAD):
        send_edge(*ORDER[n], 0)
        send_edge(*ORDER[n], 1)

    eye = lax.broadcasted_iota(jnp.int32, (128, 128), 0) == lax.broadcasted_iota(jnp.int32, (128, 128), 1)

    @pl.loop(0, 16, unroll=2)
    def _(n):
        turned = coup_ref[n].T
        row_abs[pl.ds(n, 1)] = jnp.sum(jnp.abs(turned), axis=0, keepdims=True)
        diag[pl.ds(n, 1)] = jnp.sum(jnp.where(eye, turned, 0.0), axis=0, keepdims=True)
        blocks[n] = jnp.concatenate(halves(turned), axis=1)

    def bounds_of(s, ends):
        top, low = ends
        for l in range(2):
            first = index_ref[0, l, s]
            middle = diag[pl.ds(first, 1)]
            center = middle + pot_ref[l, pl.ds(s, 1)]
            radius = row_abs[pl.ds(first, 1)] - jnp.abs(middle)
            rest = row_abs[pl.ds(index_ref[1, l, s], 1)]
            for slot in range(2, 7):
                rest = rest + row_abs[pl.ds(index_ref[slot, l, s], 1)]
            radius = radius + rest
            top = jnp.maximum(top, center + radius)
            low = jnp.maximum(low, radius - center)
        return top, low

    least = jnp.full((1, 128), -3e38, F32)
    top, low = lax.fori_loop(0, 16, bounds_of, (least, least))
    zb[z] = jnp.concatenate([jnp.broadcast_to(top, (8, 128)), jnp.broadcast_to(low, (8, 128))], axis=0)

    def exchange(buf, at, group):
        started = [send(buf.at[at], buf.at[at], *sems(), peer) for peer in group]
        copies.extend(started)
        return started

    def merged(buf, started):
        for copy in started:
            copy.wait_recv()
        best = buf[0]
        for i in range(1, buf.shape[0]):
            best = jnp.maximum(best, buf[i])
        return best

    def local_part(k, c):
        @pl.loop(0, 16, unroll=4)
        def _(s):
            for l in range(2):
                sources = [(l, s)]
                for slot in range(1, 5):
                    sources.append((l, (s + offset_ref[slot - 1, l, s]) & 15))
                slots = [0, 1, 2, 3, 4, 6 - l]
                sources.append((1 - l, (s + offset_ref[5 - l, l, s]) & 15))
                lhs = jnp.concatenate([stack[k][c][at] for at in sources], axis=1)
                rhs = jnp.concatenate([blocks[index_ref[slot, l, s]] for slot in slots], axis=0)
                partial[l, s] = product(lhs, rhs)

    def finish(k, c, part, middle, inverse):
        size = WIDTH // parts_of(k, c)
        at = slice(size * part, size * part + size)
        for l in range(2):
            edge[k, c, l, part].wait_recv()

            @pl.loop(0, 16, unroll=8)
            def _(s):
                slot = 5 + l
                outer = halo[k, c, l, part][(s + offset_ref[slot - 1, l, s]) & 15]
                total = partial[l, s, at] + product(both_halves(outer), blocks[index_ref[slot, l, s]])
                own = field[k][c][l, s, at]
                new = (total + (pot_ref[l, pl.ds(s, 1)] - middle) * own) * inverse
                if k > 0:
                    new = 2.0 * new - field[k - 1][c][l, s, at]
                if k < 2:
                    field[k + 1][c][l, s] = new
                    stack[k + 1][c][l, s] = both_halves(new)
                else:
                    d = degree[WIDTH * c + size * part : WIDTH * c + size * part + size]
                    chosen[c][s, l, at] = jnp.where(d == 1, field[1][c][l, s, at], jnp.where(d == 2, own, new))

    started = exchange(zb, z, z_peers)
    degree[...] = jnp.broadcast_to(deg_ref[...].astype(F32), (128, 128)).T.astype(jnp.int32)
    local_part(0, 0)
    xb[xx] = merged(zb, started)
    started = exchange(xb, xx, x_peers)
    best = merged(xb, started)
    yb[ylo] = best
    started = exchange(yb, ylo, [y_peer])
    best = merged(yb, started)
    upper = jnp.max(best[:8], axis=1, keepdims=True)[:1]
    lower = -jnp.max(best[8:], axis=1, keepdims=True)[:1]
    cut_edge = lower + cut_share * (upper - lower)
    middle = jnp.broadcast_to((upper + cut_edge) / 2.0, (1, 128))
    inverse = jnp.broadcast_to(2.0 / (upper - cut_edge), (1, 128))

    arrivals = []

    def send_next(n):
        if n + AHEAD < len(ORDER):
            for l in range(2):
                edge[*ORDER[n], 1 - l, 0].wait_send()
                send_edge(*ORDER[n + AHEAD], l)

    def hand_out(c):
        rows = pl.ds(pl.multiple_of(128 * st + WIDTH * c, WIDTH), WIDTH)
        final = c == NCH - 1
        for j in range(4) if final else [slice(0, 4)]:
            for d in (1, 2, 3):
                first = 4 * lax.rem(st + d, 4)
                source = chosen[c].at[first + j if final else pl.ds(first, 4)]
                copy = send(source, xt_ref.at[j, :, rows], *sems(), state_peers[d - 1])
                copies.append(copy)
                arrivals.append(copy)
        for s in range(4):
            for l in range(2):
                xt_ref[s, l, rows] = chosen[c][4 * st + s, l]

    send_next(0)
    for n, (k, c) in enumerate(ORDER):
        finish(k, c, 0, middle, inverse)
        if k == 2:
            hand_out(c)
        if n + 1 < len(ORDER):
            local_part(*ORDER[n + 1])
            send_next(n + 1)
    last = len(arrivals) - 12
    for copy in arrivals[:last]:
        copy.wait_recv()
    packed = sums[0]
    for j in range(4):
        for copy in arrivals[last + 3 * j : last + 3 * j + 3]:
            copy.wait_recv()
        hi, lo = halves(jnp.concatenate([xt_ref[j, 0], xt_ref[j, 1]], axis=1))
        for row in range(4):
            here, upto = slice(128 * row, 128 * row + 128), 128 * row + 128
            block = nt(hi[here], hi[:upto]) + (nt(hi[here], lo[:upto]) + nt(lo[here], hi[:upto]))
            for col in range(row + 1):
                at = slice(128 * SLOT[row, col], 128 * SLOT[row, col] + 128)
                piece = block[:, 128 * col : 128 * col + 128]
                packed[at] = piece if j == 0 else packed[at] + piece

    def meanwhile():
        @pl.loop(0, 8)
        def _(q):
            at = pl.ds(pl.multiple_of(q * 128, 128), 128)
            for d in range(4):
                cols = slice(128 * d, 128 * d + 128)
                xh_ref[at, cols], xl_ref[at, cols] = halves(xt_ref[lax.rem(q, 4), lax.div(q, 4), cols].T)

    sum_everywhere(*sums, gram_ref, sum_peers, sems, copies, meanwhile)
    for copy in copies:
        copy.wait_send()


def partners():
    x, y, z, core = place()
    return (
        [device(lax.rem(x + d, 4), y, z, core) for d in (1, 2, 3)],
        [device(x, lax.rem(y + d, 4), z, core) for d in (1, 2, 3)],
        [device(x, y, lax.rem(z + d, 8), core) for d in range(1, 8)],
        [device(x, y, z, 1 - core)],
    )


def sum_everywhere(packed, r1, a1, ra, rb, a2, b2, ra2, rb2, zbuf, gbuf, peers, sems, copies, meanwhile):
    x, y, z, core = place()
    x_peers, y_peers, z_peers, core_peers = peers

    def spread(group, piece):
        started = [send(*piece(d), *sems(), peer) for d, peer in enumerate(group)]
        copies.extend(started)
        return started

    def arrived(started):
        for copy in started:
            copy.wait_recv()

    def total(own, parts):
        return (own + parts[0]) + (parts[1] + parts[2])

    def one(source, target, peer):
        copies.append(send(source, target, *sems(), peer))
        return copies[-1]

    def piece_a(d):
        return lax.rem(x + d, 4) * 96

    def piece_b(d):
        return 384 + lax.rem(y + d, 4) * 64

    pieces = [(piece_a(d), 96, x_peers, ra, d) for d in (1, 2, 3, 0)], [(piece_b(d), 64, y_peers, rb, d) for d in (1, 2, 3, 0)]
    pieces = [piece for pair in zip(*pieces) for piece in pair]
    landing = [
        one(packed.at[rows_at((1 - core) * 640 + at, size)], r1.at[rows_at(at, size)], core_peers[0])
        for at, size, _, _, _ in pieces
    ]
    started = []
    for copy, (at, size, group, target, d) in zip(landing, pieces):
        copy.wait_recv()
        a1[rows_at(at, size)] = packed[rows_at(core * 640 + at, size)] + r1[rows_at(at, size)]
        if d > 0:
            started.append(one(a1.at[rows_at(at, size)], target.at[d - 1], group[d - 1]))
    meanwhile()
    arrived(started)
    a2[...] = total(a1[rows_at(x * 96, 96)], ra)
    b2[...] = total(a1[rows_at(384 + y * 64, 64)], rb)
    started = spread(y_peers, lambda d: (a2.at[rows_at(lax.rem(y + d + 1, 4) * 24, 24)], ra2.at[d]))
    started += spread(x_peers, lambda d: (b2.at[rows_at(lax.rem(x + d + 1, 4) * 16, 16)], rb2.at[d]))
    arrived(started)
    zbuf[z, :24] = total(a2[rows_at(y * 24, 24)], ra2)
    zbuf[z, 24:] = total(b2[rows_at(x * 16, 16)], rb2)
    arrived(spread(z_peers, lambda d: (zbuf.at[z], zbuf.at[z])))
    whole = ((zbuf[0] + zbuf[1]) + (zbuf[2] + zbuf[3])) + ((zbuf[4] + zbuf[5]) + (zbuf[6] + zbuf[7]))
    own_a = rows_at(core * 640 + x * 96 + y * 24, 24)
    own_b = rows_at(core * 640 + 384 + y * 64 + x * 16, 16)
    gbuf[own_a] = whole[:24]
    gbuf[own_b] = whole[24:]
    started = spread(y_peers, lambda d: (gbuf.at[own_a], gbuf.at[own_a]))
    started += spread(x_peers, lambda d: (gbuf.at[own_b], gbuf.at[own_b]))
    arrived(started)

    def share(at, size, peer):
        rows = rows_at(core * 640 + at, size)
        return one(gbuf.at[rows], gbuf.at[rows], peer)

    started = []
    for d in range(3):
        started.append((share(x * 96, 96, x_peers[d]), piece_a(3 - d), 96))
        started.append((share(384 + y * 64, 64, y_peers[d]), piece_b(3 - d), 64))
    landing = [share(x * 96, 96, core_peers[0]), share(384 + y * 64, 64, core_peers[0])]
    for copy, at, size in started:
        copy.wait_recv()
        landing.append(share(at, size, core_peers[0]))
    arrived(landing)


def filtered_rows(start_states, couplings, potential, site_offsets, coupling_index, degrees):
    vmem, smem = pl.BlockSpec(memory_space=pltpu.VMEM), pl.BlockSpec(memory_space=pltpu.SMEM)
    scratch = [pltpu.VMEM((2, 16, WIDTH, 128), F32)] * (3 * NCH)
    scratch += [pltpu.VMEM((2, 16, 2 * WIDTH, 128), BF16)] * (3 * NCH)
    for k in range(3):
        for c in range(NCH):
            scratch += [pltpu.VMEM((16, WIDTH // parts_of(k, c), 128), F32)] * (2 * parts_of(k, c))
    scratch += [pltpu.VMEM((2, 16, WIDTH, 128), F32)]
    scratch += [pltpu.VMEM((16, 2, WIDTH, 128), F32)] * NCH
    scratch += [pltpu.VMEM((16, 128, 256), BF16), pltpu.VMEM((16, 128), F32), pltpu.VMEM((16, 128), F32)]
    scratch += [pltpu.VMEM((n, 16, 128), F32) for n in (8, 4, 2)]
    scratch += [pltpu.VMEM((128, 128), jnp.int32)]
    scratch += [pltpu.VMEM((4, 2, 512, 128), F32), pltpu.VMEM((1280, 128), F32)]
    scratch += [pltpu.VMEM((640, 128), F32), pltpu.VMEM((640, 128), F32)]
    scratch += [pltpu.VMEM((3, 96, 128), F32), pltpu.VMEM((3, 64, 128), F32)]
    scratch += [pltpu.VMEM((96, 128), F32), pltpu.VMEM((64, 128), F32)]
    scratch += [pltpu.VMEM((3, 24, 128), F32), pltpu.VMEM((3, 16, 128), F32), pltpu.VMEM((8, 40, 128), F32)]
    scratch += [pltpu.SemaphoreType.DMA((COPIES,))] * 2
    return pl.pallas_call(
        filter_kernel,
        out_shape=[
            jax.ShapeDtypeStruct((1280, 128), F32),
            jax.ShapeDtypeStruct((1024, 512), BF16),
            jax.ShapeDtypeStruct((1024, 512), BF16),
        ],
        in_specs=[smem, smem, vmem, vmem, vmem, vmem],
        out_specs=[vmem] * 3,
        scratch_shapes=scratch,
        compiler_params=pltpu.CompilerParams(collective_id=0, has_side_effects=True, vmem_limit_bytes=VMEM_LIMIT),
        name="filter",
    )(coupling_index.transpose(1, 0, 2), site_offsets.transpose(1, 0, 2), start_states, couplings, potential, degrees.reshape(1, 128))


def per_device(start_states, couplings, potential, site_offsets, coupling_index, degrees):
    gram, xh, xl = filtered_rows(start_states, couplings, potential, site_offsets, coupling_index, degrees)
    return orthonormalised(gram, xh, xl).reshape(2, 4, 128, 512)


def solution(mesh):
    in_specs = (
        P("blk", None, None, "states"),
        P(),
        P("blk", None, None),
        P("blk", None, None),
        P("blk", None, None),
        P("states"),
    )
    out_specs = P("blk", "states", None, None)
    return jax.shard_map(
        per_device, mesh=mesh, in_specs=in_specs, out_specs=out_specs, check_vma=False
    )
```

```python
import functools

import jax
import jax.numpy as jnp
from jax import lax
from jax.experimental import pallas as pl
from jax.experimental.pallas import tpu as pltpu
from jax.sharding import PartitionSpec as P

cut_share = 0.3

MESH = pl.DeviceIdType.MESH
F32 = jnp.float32
BF16 = jnp.bfloat16
exact = lax.Precision.HIGHEST
VMEM_LIMIT = 60 * 1024 * 1024


def place():
    b, st = lax.axis_index("blk"), lax.axis_index("states")
    z = lax.rem(b, 8)
    x = lax.rem(lax.div(b, 8), 4)
    y = lax.div(st, 2) * 2 + lax.div(b, 32)
    return x, y, z, lax.rem(st, 2)


def device(x, y, z, core):
    return ((lax.rem(y, 2) * 4 + x) * 8 + z, lax.div(y, 2) * 2 + core)


def send(src, dst, send_sem, recv_sem, peer):
    copy = pltpu.make_async_remote_copy(
        src_ref=src, dst_ref=dst, send_sem=send_sem, recv_sem=recv_sem, device_id=peer, device_id_type=MESH
    )
    copy.start()
    return copy


def rows_at(start, size):
    return pl.ds(pl.multiple_of(start, 8), size)


def nt(a, b):
    return lax.dot_general(a, b, (((1,), (1,)), ((), ())), preferred_element_type=F32)


PAIRS = [(i, j) for i in range(4) for j in range(i + 1)]
SLOT = {pair: n for n, pair in enumerate(PAIRS)}


def halves(v):
    hi = v.astype(BF16)
    return hi, (v - hi.astype(F32)).astype(BF16)


def thirds(v):
    hi = v.astype(BF16).astype(F32)
    rest = v - hi
    mid = rest.astype(BF16).astype(F32)
    return hi, mid, rest - mid


def dot_nt(a, b):
    h, m, l = thirds(a)
    u, v, w = thirds(b)
    lhs = jnp.concatenate([h, h, m, m, h, l], axis=1).astype(BF16)
    rhs = jnp.concatenate([u, v, u, v, w, u], axis=1).astype(BF16)
    return lax.dot_general(lhs, rhs, (((1,), (1,)), ((), ())), preferred_element_type=F32)


def dot_nn(a, b):
    h, m, l = thirds(a)
    u, v, w = thirds(b)
    lhs = jnp.concatenate([h, h, m, m, h, l], axis=1).astype(BF16)
    rhs = jnp.concatenate([u, v, u, v, w, u], axis=0).astype(BF16)
    return lax.dot_general(lhs, rhs, (((1,), (0,)), ((), ())), preferred_element_type=F32)


def eliminate(work, others):
    row = lax.broadcasted_iota(jnp.int32, (16, 128), 0)

    def spread(v, rows=16):
        return jnp.broadcast_to(v, (rows, 128))

    def steps(lo, count):
        left, right = work[lo : lo + 16, :128], work[lo : lo + 16, 128:]
        cols = [spread(left[:, lo + c : lo + c + 1]) for c in range(16)]
        below = []
        for t in range(1, count):
            l2, r2 = work[lo + 16 * t : lo + 16 * t + 16, :128], work[lo + 16 * t : lo + 16 * t + 16, 128:]
            below.append([l2, r2, [spread(l2[:, lo + c : lo + c + 1]) for c in range(16)]])
        for j in range(16):
            scale = lax.rsqrt(jnp.broadcast_to(cols[j][j : j + 1, :], (8, 128)))
            scale = jnp.concatenate([scale] * 2, axis=0)
            factor = jnp.where(row > j, cols[j] * scale, 0.0)
            lrow = spread(left[j : j + 1, :]) * scale
            rrow = spread(right[j : j + 1, :]) * scale
            lower = [part[2][j] * scale for part in below]
            for c in range(j + 1, 16):
                across = spread(cols[c][j : j + 1, :]) * scale
                cols[c] = cols[c] - factor * across
                for part, f in zip(below, lower):
                    part[2][c] = part[2][c] - f * across
            left = jnp.where(row == j, lrow, left - factor * lrow)
            right = jnp.where(row == j, rrow, right - factor * rrow)
            for part, f in zip(below, lower):
                part[0] = part[0] - f * lrow
                part[1] = part[1] - f * rrow
        work[lo : lo + 16, :128] = left
        work[lo : lo + 16, 128:] = right
        for t in range(1, count):
            work[lo + 16 * t : lo + 16 * t + 16, :128] = below[t - 1][0]
            work[lo + 16 * t : lo + 16 * t + 16, 128:] = below[t - 1][1]

    for p in range(128 // PANEL):
        lo = PANEL * p
        for t in range(PANEL // 16):
            steps(lo + 16 * t, PANEL // 16 - t)
            if others:
                others.pop(0)()
        if lo + PANEL < 128:
            h, m, l = thirds(work[lo : lo + PANEL, :])
            lhs = jnp.concatenate([h[:, :128], h[:, :128], m[:, :128], m[:, :128], h[:, :128], l[:, :128]], axis=0).astype(BF16)
            rhs = jnp.concatenate([h, m, h, m, l, h], axis=0).astype(BF16)
            change = lax.dot_general(lhs, rhs, (((0,), (0,)), ((), ())), preferred_element_type=F32)
            work[lo + PANEL :, :] = work[lo + PANEL :, :] - change[lo + PANEL :, :]


PANEL = 32


def factor_kernel(g_ref, xh, xl, out_ref, blocks, work, low, inv):
    blocks[...] = g_ref[...]
    inv[...] = jnp.zeros_like(inv)
    eye = (lax.broadcasted_iota(jnp.int32, (128, 128), 0) == lax.broadcasted_iota(jnp.int32, (128, 128), 1)).astype(F32)

    def lower_block(i, n):
        low[128 * i : 128 * i + 128, 128 * n : 128 * n + 128] = dot_nt(blocks[SLOT[i, n]], work[n, :, 128:])

    def update(i, j, n):
        cols = slice(128 * n, 128 * n + 128)
        blocks[SLOT[i, j]] = blocks[SLOT[i, j]] - dot_nt(
            low[128 * i : 128 * i + 128, cols], low[128 * j : 128 * j + 128, cols]
        )

    def inverse_row(n):
        here = slice(128 * n, 128 * n + 128)
        w = work[n, :, 128:]
        inv[here, here] = w
        if n > 0:
            inv[here, : 128 * n] = -dot_nn(w, dot_nn(low[here, : 128 * n], inv[: 128 * n, : 128 * n]))

    def product_block(n, part):
        here, upto, rows = slice(128 * n, 128 * n + 128), 128 * n + 128, slice(512 * part, 512 * part + 512)
        u, v = halves(inv[here, :upto])
        a, b = xh[rows, :upto], xl[rows, :upto]
        out_ref[rows, here] = nt(a, u) + (nt(a, v) + nt(b, u))

    call = functools.partial
    others = []
    for n in range(4):
        mine = work.at[n]
        mine[:, :128] = blocks[SLOT[n, n]]
        mine[:, 128:] = eye
        eliminate(mine, others)
        while others:
            others.pop(0)()
        if n < 3:
            lower_block(n + 1, n)
            update(n + 1, n + 1, n)
        others = [call(lower_block, i, n) for i in range(n + 2, 4)]
        others += [call(update, i, j, n) for j in range(n + 1, 4) for i in range(max(j, n + 2), 4)]
        others += [call(inverse_row, n), call(product_block, n, 0), call(product_block, n, 1)]
    for other in others:
        other()


def orthonormalised(packed, xh, xl):
    vmem = pl.BlockSpec(memory_space=pltpu.VMEM)
    return pl.pallas_call(
        factor_kernel,
        out_shape=jax.ShapeDtypeStruct((1024, 512), F32),
        in_specs=[vmem] * 3,
        out_specs=vmem,
        scratch_shapes=[
            pltpu.VMEM((10, 128, 128), F32),
            pltpu.VMEM((4, 128, 256), F32),
            pltpu.VMEM((512, 512), F32),
            pltpu.VMEM((512, 512), F32),
        ],
        compiler_params=pltpu.CompilerParams(vmem_limit_bytes=VMEM_LIMIT),
        name="factor",
    )(packed.reshape(10, 128, 128), xh, xl)


NCH = 2
WIDTH = 128 // NCH
PARTS = 1
AHEAD = 1
ORDER = [(k, c) for k in range(3) for c in range(NCH)]
COPIES = 6 * NCH + 2 * (PARTS - 1) + 3 * (NCH + PARTS - 1) + 9 + 11 + 47


def both_halves(v):
    hi, lo = halves(v)
    return jnp.concatenate([hi, lo], axis=0)


def product(lhs, rhs):
    full = lax.dot_general(lhs, rhs, (((1,), (0,)), ((), ())), preferred_element_type=F32)
    half = full.shape[0] // 2
    return (full[:half, :128] + full[half:, :128]) + (full[:half, 128:] + full[half:, 128:])


def parts_of(k, c):
    return PARTS if (k, c) == (2, NCH - 1) else 1


def filter_kernel(index_ref, offset_ref, start_ref, coup_ref, pot_ref, deg_ref, gram_ref, xh_ref, xl_ref, *scratch):
    scratch = iter(scratch)
    field = [[next(scratch) for _ in range(NCH)] for _ in range(3)]
    stack = [[next(scratch) for _ in range(NCH)] for _ in range(3)]
    halo = {}
    for k in range(3):
        for c in range(NCH):
            for part in range(parts_of(k, c)):
                for l in range(2):
                    halo[k, c, l, part] = next(scratch)
    partial = next(scratch)
    chosen = [next(scratch) for _ in range(NCH)]
    blocks, row_abs, diag = next(scratch), next(scratch), next(scratch)
    zb, xb, yb = next(scratch), next(scratch), next(scratch)
    degree = next(scratch)
    xt_ref = next(scratch)
    sums = [next(scratch) for _ in range(10)]
    send_sems, recv_sems = next(scratch), next(scratch)
    used = iter(range(COPIES))

    def sems():
        i = next(used)
        return send_sems.at[i], recv_sems.at[i]

    b, st = lax.axis_index("blk"), lax.axis_index("states")
    z, xx, ylo = lax.rem(b, 8), lax.rem(lax.div(b, 8), 4), lax.div(b, 32)
    left, right = (lax.rem(b + 63, 64), st), (lax.rem(b + 1, 64), st)
    z_peers = [(b - z + lax.rem(z + d, 8), st) for d in range(1, 8)]
    x_peers = [(b - xx * 8 + lax.rem(xx + d, 4) * 8, st) for d in range(1, 4)]
    y_peer = (lax.rem(b + 32, 64), st)
    state_peers = [(b, lax.rem(st + d, 4)) for d in range(1, 4)]
    sum_peers = partners()
    peers = [left, right, y_peer] + z_peers + x_peers + state_peers + [peer for group in sum_peers for peer in group]
    barrier = pltpu.get_barrier_semaphore()
    for peer in peers:
        pl.semaphore_signal(barrier, inc=1, device_id=peer, device_id_type=MESH)

    @pl.loop(0, 16, unroll=2)
    def _(s):
        for l in range(2):
            turned = start_ref[l, s].T
            for c in range(NCH):
                part = turned[WIDTH * c : WIDTH * c + WIDTH]
                field[0][c][l, s] = part
                stack[0][c][l, s] = both_halves(part)

    pl.semaphore_wait(barrier, len(peers))
    copies = []
    edge = {}

    def send_edge(k, c, l):
        size = WIDTH // parts_of(k, c)
        for part in range(parts_of(k, c)):
            source = field[k][c].at[l, :, size * part : size * part + size]
            copy = send(source, halo[k, c, 1 - l, part], *sems(), right if l else left)
            if ORDER.index((k, c)) + AHEAD >= len(ORDER):
                copies.append(copy)
            edge[k, c, 1 - l, part] = copy

    for n in range(AHEAD):
        send_edge(*ORDER[n], 0)
        send_edge(*ORDER[n], 1)

    eye = lax.broadcasted_iota(jnp.int32, (128, 128), 0) == lax.broadcasted_iota(jnp.int32, (128, 128), 1)

    @pl.loop(0, 16, unroll=2)
    def _(n):
        turned = coup_ref[n].T
        row_abs[pl.ds(n, 1)] = jnp.sum(jnp.abs(turned), axis=0, keepdims=True)
        diag[pl.ds(n, 1)] = jnp.sum(jnp.where(eye, turned, 0.0), axis=0, keepdims=True)
        blocks[n] = jnp.concatenate(halves(turned), axis=1)

    def bounds_of(s, ends):
        top, low = ends
        for l in range(2):
            first = index_ref[0, l, s]
            middle = diag[pl.ds(first, 1)]
            center = middle + pot_ref[l, pl.ds(s, 1)]
            radius = row_abs[pl.ds(first, 1)] - jnp.abs(middle)
            rest = row_abs[pl.ds(index_ref[1, l, s], 1)]
            for slot in range(2, 7):
                rest = rest + row_abs[pl.ds(index_ref[slot, l, s], 1)]
            radius = radius + rest
            top = jnp.maximum(top, center + radius)
            low = jnp.maximum(low, radius - center)
        return top, low

    least = jnp.full((1, 128), -3e38, F32)
    top, low = lax.fori_loop(0, 16, bounds_of, (least, least))
    zb[z] = jnp.concatenate([jnp.broadcast_to(top, (8, 128)), jnp.broadcast_to(low, (8, 128))], axis=0)

    def exchange(buf, at, group):
        started = [send(buf.at[at], buf.at[at], *sems(), peer) for peer in group]
        copies.extend(started)
        return started

    def merged(buf, started):
        for copy in started:
            copy.wait_recv()
        best = buf[0]
        for i in range(1, buf.shape[0]):
            best = jnp.maximum(best, buf[i])
        return best

    def local_part(k, c):
        @pl.loop(0, 16, unroll=4)
        def _(s):
            for l in range(2):
                sources = [(l, s)]
                for slot in range(1, 5):
                    sources.append((l, (s + offset_ref[slot - 1, l, s]) & 15))
                slots = [0, 1, 2, 3, 4, 6 - l]
                sources.append((1 - l, (s + offset_ref[5 - l, l, s]) & 15))
                lhs = jnp.concatenate([stack[k][c][at] for at in sources], axis=1)
                rhs = jnp.concatenate([blocks[index_ref[slot, l, s]] for slot in slots], axis=0)
                partial[l, s] = product(lhs, rhs)

    def finish(k, c, part, middle, inverse):
        size = WIDTH // parts_of(k, c)
        at = slice(size * part, size * part + size)
        for l in range(2):
            edge[k, c, l, part].wait_recv()

            @pl.loop(0, 16, unroll=8)
            def _(s):
                slot = 5 + l
                outer = halo[k, c, l, part][(s + offset_ref[slot - 1, l, s]) & 15]
                total = partial[l, s, at] + product(both_halves(outer), blocks[index_ref[slot, l, s]])
                own = field[k][c][l, s, at]
                new = (total + (pot_ref[l, pl.ds(s, 1)] - middle) * own) * inverse
                if k > 0:
                    new = 2.0 * new - field[k - 1][c][l, s, at]
                if k < 2:
                    field[k + 1][c][l, s] = new
                    stack[k + 1][c][l, s] = both_halves(new)
                else:
                    d = degree[WIDTH * c + size * part : WIDTH * c + size * part + size]
                    chosen[c][s, l, at] = jnp.where(d == 1, field[1][c][l, s, at], jnp.where(d == 2, own, new))

    started = exchange(zb, z, z_peers)
    degree[...] = jnp.broadcast_to(deg_ref[...].astype(F32), (128, 128)).T.astype(jnp.int32)
    local_part(0, 0)
    xb[xx] = merged(zb, started)
    started = exchange(xb, xx, x_peers)
    best = merged(xb, started)
    yb[ylo] = best
    started = exchange(yb, ylo, [y_peer])
    best = merged(yb, started)
    upper = jnp.max(best[:8], axis=1, keepdims=True)[:1]
    lower = -jnp.max(best[8:], axis=1, keepdims=True)[:1]
    cut_edge = lower + cut_share * (upper - lower)
    middle = jnp.broadcast_to((upper + cut_edge) / 2.0, (1, 128))
    inverse = jnp.broadcast_to(2.0 / (upper - cut_edge), (1, 128))

    arrivals = []

    def send_next(n):
        if n + AHEAD < len(ORDER):
            for l in range(2):
                edge[*ORDER[n], 1 - l, 0].wait_send()
                send_edge(*ORDER[n + AHEAD], l)

    def hand_out(c):
        rows = pl.ds(pl.multiple_of(128 * st + WIDTH * c, WIDTH), WIDTH)
        final = c == NCH - 1
        for j in range(4) if final else [slice(0, 4)]:
            for d in (1, 2, 3):
                first = 4 * lax.rem(st + d, 4)
                source = chosen[c].at[first + j if final else pl.ds(first, 4)]
                copy = send(source, xt_ref.at[j, :, rows], *sems(), state_peers[d - 1])
                copies.append(copy)
                arrivals.append(copy)
        for s in range(4):
            for l in range(2):
                xt_ref[s, l, rows] = chosen[c][4 * st + s, l]

    send_next(0)
    for n, (k, c) in enumerate(ORDER):
        finish(k, c, 0, middle, inverse)
        if k == 2:
            hand_out(c)
        if n + 1 < len(ORDER):
            local_part(*ORDER[n + 1])
            send_next(n + 1)
    last = len(arrivals) - 12
    for copy in arrivals[:last]:
        copy.wait_recv()
    packed = sums[0]
    for j in range(4):
        for copy in arrivals[last + 3 * j : last + 3 * j + 3]:
            copy.wait_recv()
        hi, lo = halves(jnp.concatenate([xt_ref[j, 0], xt_ref[j, 1]], axis=1))
        for row in range(4):
            here, upto = slice(128 * row, 128 * row + 128), 128 * row + 128
            block = nt(hi[here], hi[:upto]) + (nt(hi[here], lo[:upto]) + nt(lo[here], hi[:upto]))
            for col in range(row + 1):
                at = slice(128 * SLOT[row, col], 128 * SLOT[row, col] + 128)
                piece = block[:, 128 * col : 128 * col + 128]
                packed[at] = piece if j == 0 else packed[at] + piece

    def meanwhile(part):
        @pl.loop(4 * part, 4 * part + 4, unroll=2)
        def _(q):
            at = pl.ds(pl.multiple_of(q * 128, 128), 128)
            for d in range(4):
                cols = slice(128 * d, 128 * d + 128)
                xh_ref[at, cols], xl_ref[at, cols] = halves(xt_ref[lax.rem(q, 4), lax.div(q, 4), cols].T)

    sum_everywhere(*sums, gram_ref, sum_peers, sems, copies, meanwhile)
    for copy in copies:
        copy.wait_send()


def partners():
    x, y, z, core = place()
    return (
        [device(lax.rem(x + d, 4), y, z, core) for d in (1, 2, 3)],
        [device(x, lax.rem(y + d, 4), z, core) for d in (1, 2, 3)],
        [device(x, y, lax.rem(z + d, 8), core) for d in range(1, 8)],
        [device(x, y, z, 1 - core)],
    )


def sum_everywhere(packed, r1, a1, ra, rb, a2, b2, ra2, rb2, zbuf, gbuf, peers, sems, copies, meanwhile):
    x, y, z, core = place()
    x_peers, y_peers, z_peers, core_peers = peers

    def spread(group, piece):
        started = [send(*piece(d), *sems(), peer) for d, peer in enumerate(group)]
        copies.extend(started)
        return started

    def arrived(started):
        for copy in started:
            copy.wait_recv()

    def total(own, parts):
        return (own + parts[0]) + (parts[1] + parts[2])

    def one(source, target, peer):
        copies.append(send(source, target, *sems(), peer))
        return copies[-1]

    def piece_a(d):
        return lax.rem(x + d, 4) * 96

    def piece_b(d):
        return 384 + lax.rem(y + d, 4) * 64

    pieces = [(piece_a(d), 96, x_peers, ra, d) for d in (1, 2, 3, 0)], [(piece_b(d), 64, y_peers, rb, d) for d in (1, 2, 3, 0)]
    pieces = [piece for pair in zip(*pieces) for piece in pair]
    landing = [
        one(packed.at[rows_at((1 - core) * 640 + at, size)], r1.at[rows_at(at, size)], core_peers[0])
        for at, size, _, _, _ in pieces
    ]
    started = []
    for copy, (at, size, group, target, d) in zip(landing, pieces):
        copy.wait_recv()
        a1[rows_at(at, size)] = packed[rows_at(core * 640 + at, size)] + r1[rows_at(at, size)]
        if d > 0:
            started.append(one(a1.at[rows_at(at, size)], target.at[d - 1], group[d - 1]))
    meanwhile(0)
    arrived(started)
    a2[...] = total(a1[rows_at(x * 96, 96)], ra)
    b2[...] = total(a1[rows_at(384 + y * 64, 64)], rb)
    started = spread(y_peers, lambda d: (a2.at[rows_at(lax.rem(y + d + 1, 4) * 24, 24)], ra2.at[d]))
    started += spread(x_peers, lambda d: (b2.at[rows_at(lax.rem(x + d + 1, 4) * 16, 16)], rb2.at[d]))
    arrived(started)
    zbuf[z, :24] = total(a2[rows_at(y * 24, 24)], ra2)
    zbuf[z, 24:] = total(b2[rows_at(x * 16, 16)], rb2)
    started = spread(z_peers, lambda d: (zbuf.at[z], zbuf.at[z]))
    meanwhile(1)
    arrived(started)
    whole = ((zbuf[0] + zbuf[1]) + (zbuf[2] + zbuf[3])) + ((zbuf[4] + zbuf[5]) + (zbuf[6] + zbuf[7]))
    own_a = rows_at(core * 640 + x * 96 + y * 24, 24)
    own_b = rows_at(core * 640 + 384 + y * 64 + x * 16, 16)
    gbuf[own_a] = whole[:24]
    gbuf[own_b] = whole[24:]
    started = spread(y_peers, lambda d: (gbuf.at[own_a], gbuf.at[own_a]))
    started += spread(x_peers, lambda d: (gbuf.at[own_b], gbuf.at[own_b]))
    arrived(started)

    def share(at, size, peer):
        rows = rows_at(core * 640 + at, size)
        return one(gbuf.at[rows], gbuf.at[rows], peer)

    started = []
    for d in range(3):
        started.append((share(x * 96, 96, x_peers[d]), piece_a(3 - d), 96))
        started.append((share(384 + y * 64, 64, y_peers[d]), piece_b(3 - d), 64))
    landing = [share(x * 96, 96, core_peers[0]), share(384 + y * 64, 64, core_peers[0])]
    for copy, at, size in started:
        copy.wait_recv()
        landing.append(share(at, size, core_peers[0]))
    arrived(landing)


def filtered_rows(start_states, couplings, potential, site_offsets, coupling_index, degrees):
    vmem, smem = pl.BlockSpec(memory_space=pltpu.VMEM), pl.BlockSpec(memory_space=pltpu.SMEM)
    scratch = [pltpu.VMEM((2, 16, WIDTH, 128), F32)] * (3 * NCH)
    scratch += [pltpu.VMEM((2, 16, 2 * WIDTH, 128), BF16)] * (3 * NCH)
    for k in range(3):
        for c in range(NCH):
            scratch += [pltpu.VMEM((16, WIDTH // parts_of(k, c), 128), F32)] * (2 * parts_of(k, c))
    scratch += [pltpu.VMEM((2, 16, WIDTH, 128), F32)]
    scratch += [pltpu.VMEM((16, 2, WIDTH, 128), F32)] * NCH
    scratch += [pltpu.VMEM((16, 128, 256), BF16), pltpu.VMEM((16, 128), F32), pltpu.VMEM((16, 128), F32)]
    scratch += [pltpu.VMEM((n, 16, 128), F32) for n in (8, 4, 2)]
    scratch += [pltpu.VMEM((128, 128), jnp.int32)]
    scratch += [pltpu.VMEM((4, 2, 512, 128), F32), pltpu.VMEM((1280, 128), F32)]
    scratch += [pltpu.VMEM((640, 128), F32), pltpu.VMEM((640, 128), F32)]
    scratch += [pltpu.VMEM((3, 96, 128), F32), pltpu.VMEM((3, 64, 128), F32)]
    scratch += [pltpu.VMEM((96, 128), F32), pltpu.VMEM((64, 128), F32)]
    scratch += [pltpu.VMEM((3, 24, 128), F32), pltpu.VMEM((3, 16, 128), F32), pltpu.VMEM((8, 40, 128), F32)]
    scratch += [pltpu.SemaphoreType.DMA((COPIES,))] * 2
    return pl.pallas_call(
        filter_kernel,
        out_shape=[
            jax.ShapeDtypeStruct((1280, 128), F32),
            jax.ShapeDtypeStruct((1024, 512), BF16),
            jax.ShapeDtypeStruct((1024, 512), BF16),
        ],
        in_specs=[smem, smem, vmem, vmem, vmem, vmem],
        out_specs=[vmem] * 3,
        scratch_shapes=scratch,
        compiler_params=pltpu.CompilerParams(collective_id=0, has_side_effects=True, vmem_limit_bytes=VMEM_LIMIT),
        name="filter",
    )(coupling_index.transpose(1, 0, 2), site_offsets.transpose(1, 0, 2), start_states, couplings, potential, degrees.reshape(1, 128))


def per_device(start_states, couplings, potential, site_offsets, coupling_index, degrees):
    gram, xh, xl = filtered_rows(start_states, couplings, potential, site_offsets, coupling_index, degrees)
    return orthonormalised(gram, xh, xl).reshape(2, 4, 128, 512)


def solution(mesh):
    in_specs = (
        P("blk", None, None, "states"),
        P(),
        P("blk", None, None),
        P("blk", None, None),
        P("blk", None, None),
        P("states"),
    )
    out_specs = P("blk", "states", None, None)
    return jax.shard_map(
        per_device, mesh=mesh, in_specs=in_specs, out_specs=out_specs, check_vma=False
    )
```

```python
import functools

import jax
import jax.numpy as jnp
from jax import lax
from jax.experimental import pallas as pl
from jax.experimental.pallas import tpu as pltpu
from jax.sharding import PartitionSpec as P

cut_share = 0.3

MESH = pl.DeviceIdType.MESH
F32 = jnp.float32
BF16 = jnp.bfloat16
exact = lax.Precision.HIGHEST
VMEM_LIMIT = 60 * 1024 * 1024


def place():
    b, st = lax.axis_index("blk"), lax.axis_index("states")
    z = lax.rem(b, 8)
    x = lax.rem(lax.div(b, 8), 4)
    y = lax.div(st, 2) * 2 + lax.div(b, 32)
    return x, y, z, lax.rem(st, 2)


def device(x, y, z, core):
    return ((lax.rem(y, 2) * 4 + x) * 8 + z, lax.div(y, 2) * 2 + core)


def send(src, dst, send_sem, recv_sem, peer):
    copy = pltpu.make_async_remote_copy(
        src_ref=src, dst_ref=dst, send_sem=send_sem, recv_sem=recv_sem, device_id=peer, device_id_type=MESH
    )
    copy.start()
    return copy


def rows_at(start, size):
    return pl.ds(pl.multiple_of(start, 8), size)


def nt(a, b):
    return lax.dot_general(a, b, (((1,), (1,)), ((), ())), preferred_element_type=F32)


PAIRS = [(i, j) for i in range(4) for j in range(i + 1)]
SLOT = {pair: n for n, pair in enumerate(PAIRS)}


def halves(v):
    hi = v.astype(BF16)
    return hi, (v - hi.astype(F32)).astype(BF16)


def thirds(v):
    hi = v.astype(BF16).astype(F32)
    rest = v - hi
    mid = rest.astype(BF16).astype(F32)
    return hi, mid, rest - mid


def dot_nt(a, b):
    h, m, l = thirds(a)
    u, v, w = thirds(b)
    lhs = jnp.concatenate([h, h, m, m, h, l], axis=1).astype(BF16)
    rhs = jnp.concatenate([u, v, u, v, w, u], axis=1).astype(BF16)
    return lax.dot_general(lhs, rhs, (((1,), (1,)), ((), ())), preferred_element_type=F32)


def dot_nn(a, b):
    h, m, l = thirds(a)
    u, v, w = thirds(b)
    lhs = jnp.concatenate([h, h, m, m, h, l], axis=1).astype(BF16)
    rhs = jnp.concatenate([u, v, u, v, w, u], axis=0).astype(BF16)
    return lax.dot_general(lhs, rhs, (((1,), (0,)), ((), ())), preferred_element_type=F32)


def eliminate(work, others):
    row = lax.broadcasted_iota(jnp.int32, (16, 128), 0)

    def spread(v, rows=16):
        return jnp.broadcast_to(v, (rows, 128))

    def steps(lo, count):
        left, right = work[lo : lo + 16, :128], work[lo : lo + 16, 128:]
        cols = [spread(left[:, lo + c : lo + c + 1]) for c in range(16)]
        below = []
        for t in range(1, count):
            l2, r2 = work[lo + 16 * t : lo + 16 * t + 16, :128], work[lo + 16 * t : lo + 16 * t + 16, 128:]
            below.append([l2, r2, [spread(l2[:, lo + c : lo + c + 1]) for c in range(16)]])
        for j in range(16):
            scale = lax.rsqrt(jnp.broadcast_to(cols[j][j : j + 1, :], (8, 128)))
            scale = jnp.concatenate([scale] * 2, axis=0)
            factor = jnp.where(row > j, cols[j] * scale, 0.0)
            lrow = spread(left[j : j + 1, :]) * scale
            rrow = spread(right[j : j + 1, :]) * scale
            lower = [part[2][j] * scale for part in below]
            for c in range(j + 1, 16):
                across = spread(cols[c][j : j + 1, :]) * scale
                cols[c] = cols[c] - factor * across
                for part, f in zip(below, lower):
                    part[2][c] = part[2][c] - f * across
            left = jnp.where(row == j, lrow, left - factor * lrow)
            right = jnp.where(row == j, rrow, right - factor * rrow)
            for part, f in zip(below, lower):
                part[0] = part[0] - f * lrow
                part[1] = part[1] - f * rrow
        work[lo : lo + 16, :128] = left
        work[lo : lo + 16, 128:] = right
        for t in range(1, count):
            work[lo + 16 * t : lo + 16 * t + 16, :128] = below[t - 1][0]
            work[lo + 16 * t : lo + 16 * t + 16, 128:] = below[t - 1][1]

    for p in range(128 // PANEL):
        lo = PANEL * p
        for t in range(PANEL // 16):
            steps(lo + 16 * t, PANEL // 16 - t)
            if others:
                others.pop(0)()
        if lo + PANEL < 128:
            h, m, l = thirds(work[lo : lo + PANEL, :])
            lhs = jnp.concatenate([h[:, :128], h[:, :128], m[:, :128], m[:, :128], h[:, :128], l[:, :128]], axis=0).astype(BF16)
            rhs = jnp.concatenate([h, m, h, m, l, h], axis=0).astype(BF16)
            change = lax.dot_general(lhs, rhs, (((0,), (0,)), ((), ())), preferred_element_type=F32)
            work[lo + PANEL :, :] = work[lo + PANEL :, :] - change[lo + PANEL :, :]


PANEL = 32


def factor_kernel(g_ref, xh, xl, out_ref, blocks, work, low, inv):
    blocks[...] = g_ref[...]
    inv[...] = jnp.zeros_like(inv)
    eye = (lax.broadcasted_iota(jnp.int32, (128, 128), 0) == lax.broadcasted_iota(jnp.int32, (128, 128), 1)).astype(F32)

    def lower_block(i, n):
        low[128 * i : 128 * i + 128, 128 * n : 128 * n + 128] = dot_nt(blocks[SLOT[i, n]], work[n, :, 128:])

    def update(i, j, n):
        cols = slice(128 * n, 128 * n + 128)
        blocks[SLOT[i, j]] = blocks[SLOT[i, j]] - dot_nt(
            low[128 * i : 128 * i + 128, cols], low[128 * j : 128 * j + 128, cols]
        )

    def inverse_row(n):
        here = slice(128 * n, 128 * n + 128)
        w = work[n, :, 128:]
        inv[here, here] = w
        if n > 0:
            inv[here, : 128 * n] = -dot_nn(w, dot_nn(low[here, : 128 * n], inv[: 128 * n, : 128 * n]))

    def product_block(n, part):
        here, upto, rows = slice(128 * n, 128 * n + 128), 128 * n + 128, slice(512 * part, 512 * part + 512)
        u, v = halves(inv[here, :upto])
        a, b = xh[rows, :upto], xl[rows, :upto]
        out_ref[rows, here] = nt(a, u) + (nt(a, v) + nt(b, u))

    call = functools.partial
    others = []
    for n in range(4):
        mine = work.at[n]
        mine[:, :128] = blocks[SLOT[n, n]]
        mine[:, 128:] = eye
        eliminate(mine, others)
        while others:
            others.pop(0)()
        if n < 3:
            lower_block(n + 1, n)
            update(n + 1, n + 1, n)
        others = [call(lower_block, i, n) for i in range(n + 2, 4)]
        others += [call(update, i, j, n) for j in range(n + 1, 4) for i in range(max(j, n + 2), 4)]
        others += [call(inverse_row, n), call(product_block, n, 0), call(product_block, n, 1)]
    for other in others:
        other()


def orthonormalised(packed, xh, xl):
    vmem = pl.BlockSpec(memory_space=pltpu.VMEM)
    return pl.pallas_call(
        factor_kernel,
        out_shape=jax.ShapeDtypeStruct((1024, 512), F32),
        in_specs=[vmem] * 3,
        out_specs=vmem,
        scratch_shapes=[
            pltpu.VMEM((10, 128, 128), F32),
            pltpu.VMEM((4, 128, 256), F32),
            pltpu.VMEM((512, 512), F32),
            pltpu.VMEM((512, 512), F32),
        ],
        compiler_params=pltpu.CompilerParams(vmem_limit_bytes=VMEM_LIMIT),
        name="factor",
    )(packed.reshape(10, 128, 128), xh, xl)


NCH = 4
WIDTH = 128 // NCH
PARTS = 1
AHEAD = 2
ORDER = [(k, c) for k in range(3) for c in range(NCH)]
COPIES = 6 * NCH + 2 * (PARTS - 1) + 3 * (NCH + PARTS - 1) + 9 + 14 + 47


def both_halves(v):
    hi, lo = halves(v)
    return jnp.concatenate([hi, lo], axis=0)


def product(lhs, rhs):
    full = lax.dot_general(lhs, rhs, (((1,), (0,)), ((), ())), preferred_element_type=F32)
    half = full.shape[0] // 2
    return (full[:half, :128] + full[half:, :128]) + (full[:half, 128:] + full[half:, 128:])


def parts_of(k, c):
    return PARTS if (k, c) == (2, NCH - 1) else 1


def filter_kernel(index_ref, offset_ref, start_ref, coup_ref, pot_ref, deg_ref, gram_ref, xh_ref, xl_ref, *scratch):
    scratch = iter(scratch)
    field = [[next(scratch) for _ in range(NCH)] for _ in range(3)]
    stack = [[next(scratch) for _ in range(NCH)] for _ in range(3)]
    halo = {}
    for k in range(3):
        for c in range(NCH):
            for part in range(parts_of(k, c)):
                for l in range(2):
                    halo[k, c, l, part] = next(scratch)
    partial = [next(scratch) for _ in range(NCH)]
    chosen = [next(scratch) for _ in range(NCH)]
    blocks, row_abs, diag = next(scratch), next(scratch), next(scratch)
    zb, plane_buf = next(scratch), next(scratch)
    degree = next(scratch)
    xt_ref = next(scratch)
    sums = [next(scratch) for _ in range(10)]
    send_sems, recv_sems = next(scratch), next(scratch)
    used = iter(range(COPIES))

    def sems():
        i = next(used)
        return send_sems.at[i], recv_sems.at[i]

    b, st = lax.axis_index("blk"), lax.axis_index("states")
    z = lax.rem(b, 8)
    left, right = (lax.rem(b + 63, 64), st), (lax.rem(b + 1, 64), st)
    z_peers = [(b - z + lax.rem(z + d, 8), st) for d in range(1, 8)]
    plane = lax.div(b, 8)
    plane_peers = [(lax.rem(plane + d, 8) * 8 + z, st) for d in range(1, 8)]
    state_peers = [(b, lax.rem(st + d, 4)) for d in range(1, 4)]
    sum_peers = partners()
    peers = [left, right] + z_peers + plane_peers + state_peers + [peer for group in sum_peers for peer in group]
    barrier = pltpu.get_barrier_semaphore()
    for peer in peers:
        pl.semaphore_signal(barrier, inc=1, device_id=peer, device_id_type=MESH)

    copies = []
    edge = {}

    def send_edge(k, c, l):
        size = WIDTH // parts_of(k, c)
        for part in range(parts_of(k, c)):
            source = field[k][c].at[l, :, size * part : size * part + size]
            copy = send(source, halo[k, c, 1 - l, part], *sems(), right if l else left)
            if ORDER.index((k, c)) + AHEAD >= len(ORDER):
                copies.append(copy)
            edge[k, c, 1 - l, part] = copy


    eye = lax.broadcasted_iota(jnp.int32, (128, 128), 0) == lax.broadcasted_iota(jnp.int32, (128, 128), 1)

    @pl.loop(0, 16, unroll=2)
    def _(n):
        turned = coup_ref[n].T
        row_abs[pl.ds(n, 1)] = jnp.sum(jnp.abs(turned), axis=0, keepdims=True)
        diag[pl.ds(n, 1)] = jnp.sum(jnp.where(eye, turned, 0.0), axis=0, keepdims=True)
        blocks[n] = jnp.concatenate(halves(turned), axis=1)

    def bounds_of(s, ends):
        top, low = ends
        for l in range(2):
            first = index_ref[0, l, s]
            middle = diag[pl.ds(first, 1)]
            center = middle + pot_ref[l, pl.ds(s, 1)]
            radius = row_abs[pl.ds(first, 1)] - jnp.abs(middle)
            rest = row_abs[pl.ds(index_ref[1, l, s], 1)]
            for slot in range(2, 7):
                rest = rest + row_abs[pl.ds(index_ref[slot, l, s], 1)]
            radius = radius + rest
            top = jnp.maximum(top, center + radius)
            low = jnp.maximum(low, radius - center)
        return top, low

    least = jnp.full((1, 128), -3e38, F32)
    top, low = lax.fori_loop(0, 16, bounds_of, (least, least))
    zb[z] = jnp.concatenate([jnp.broadcast_to(top, (8, 128)), jnp.broadcast_to(low, (8, 128))], axis=0)

    def exchange(buf, at, group):
        started = [send(buf.at[at], buf.at[at], *sems(), peer) for peer in group]
        copies.extend(started)
        return started

    def merged(buf, started):
        for copy in started:
            copy.wait_recv()
        best = buf[0]
        for i in range(1, buf.shape[0]):
            best = jnp.maximum(best, buf[i])
        return best

    def local_part(k, c):
        @pl.loop(0, 16, unroll=4)
        def _(s):
            for l in range(2):
                sources = [(l, s)]
                for slot in range(1, 5):
                    sources.append((l, (s + offset_ref[slot - 1, l, s]) & 15))
                slots = [0, 1, 2, 3, 4, 6 - l]
                sources.append((1 - l, (s + offset_ref[5 - l, l, s]) & 15))
                lhs = jnp.concatenate([stack[k][c][at] for at in sources], axis=1)
                rhs = jnp.concatenate([blocks[index_ref[slot, l, s]] for slot in slots], axis=0)
                partial[c][l, s] = product(lhs, rhs)

    def finish(k, c, part, middle, inverse):
        size = WIDTH // parts_of(k, c)
        at = slice(size * part, size * part + size)
        for l in range(2):
            edge[k, c, l, part].wait_recv()

            @pl.loop(0, 16, unroll=8)
            def _(s):
                slot = 5 + l
                outer = halo[k, c, l, part][(s + offset_ref[slot - 1, l, s]) & 15]
                total = partial[c][l, s, at] + product(both_halves(outer), blocks[index_ref[slot, l, s]])
                own = field[k][c][l, s, at]
                new = (total + (pot_ref[l, pl.ds(s, 1)] - middle) * own) * inverse
                if k > 0:
                    new = 2.0 * new - field[k - 1][c][l, s, at]
                if k < 2:
                    field[k + 1][c][l, s] = new
                    stack[k + 1][c][l, s] = both_halves(new)
                else:
                    d = degree[WIDTH * c + size * part : WIDTH * c + size * part + size]
                    chosen[c][s, l, at] = jnp.where(d == 1, field[1][c][l, s, at], jnp.where(d == 2, own, new))

    pl.semaphore_wait(barrier, len(peers))
    started = exchange(zb, z, z_peers)

    @pl.loop(0, 16, unroll=2)
    def _(s):
        for l in range(2):
            turned = start_ref[l, s].T
            for c in range(NCH):
                part = turned[WIDTH * c : WIDTH * c + WIDTH]
                field[0][c][l, s] = part
                stack[0][c][l, s] = both_halves(part)

    plane_buf[plane] = merged(zb, started)
    started = exchange(plane_buf, plane, plane_peers)
    for n in range(AHEAD):
        send_edge(*ORDER[n], 0)
        send_edge(*ORDER[n], 1)
    degree[...] = jnp.broadcast_to(deg_ref[...].astype(F32), (128, 128)).T.astype(jnp.int32)
    for c in range(NCH):
        local_part(0, c)
    best = merged(plane_buf, started)
    upper = jnp.max(best[:8], axis=1, keepdims=True)[:1]
    lower = -jnp.max(best[8:], axis=1, keepdims=True)[:1]
    cut_edge = lower + cut_share * (upper - lower)
    middle = jnp.broadcast_to((upper + cut_edge) / 2.0, (1, 128))
    inverse = jnp.broadcast_to(2.0 / (upper - cut_edge), (1, 128))

    arrivals = []

    def send_next(n):
        if n + AHEAD < len(ORDER):
            for l in range(2):
                edge[*ORDER[n], 1 - l, 0].wait_send()
                send_edge(*ORDER[n + AHEAD], l)

    def hand_out(c):
        rows = pl.ds(pl.multiple_of(128 * st + WIDTH * c, WIDTH), WIDTH)
        final = c == NCH - 1
        for j in range(4) if final else [slice(0, 4)]:
            for d in (1, 2, 3):
                first = 4 * lax.rem(st + d, 4)
                source = chosen[c].at[first + j if final else pl.ds(first, 4)]
                copy = send(source, xt_ref.at[j, :, rows], *sems(), state_peers[d - 1])
                copies.append(copy)
                arrivals.append(copy)
        for s in range(4):
            for l in range(2):
                xt_ref[s, l, rows] = chosen[c][4 * st + s, l]

    for n, (k, c) in enumerate(ORDER):
        if n == 0:
            send_next(0)
        finish(k, c, 0, middle, inverse)
        if k == 2:
            hand_out(c)
        else:
            local_part(k + 1, c)
        if n + 1 < len(ORDER):
            send_next(n + 1)
    last = len(arrivals) - 12
    for copy in arrivals[:last]:
        copy.wait_recv()
    packed = sums[0]
    for j in range(4):
        for copy in arrivals[last + 3 * j : last + 3 * j + 3]:
            copy.wait_recv()
        hi, lo = halves(jnp.concatenate([xt_ref[j, 0], xt_ref[j, 1]], axis=1))
        for row in range(4):
            here, upto = slice(128 * row, 128 * row + 128), 128 * row + 128
            block = nt(hi[here], hi[:upto]) + (nt(hi[here], lo[:upto]) + nt(lo[here], hi[:upto]))
            for col in range(row + 1):
                at = slice(128 * SLOT[row, col], 128 * SLOT[row, col] + 128)
                piece = block[:, 128 * col : 128 * col + 128]
                packed[at] = piece if j == 0 else packed[at] + piece

    def meanwhile():
        @pl.loop(0, 8)
        def _(q):
            at = pl.ds(pl.multiple_of(q * 128, 128), 128)
            for d in range(4):
                cols = slice(128 * d, 128 * d + 128)
                xh_ref[at, cols], xl_ref[at, cols] = halves(xt_ref[lax.rem(q, 4), lax.div(q, 4), cols].T)

    sum_everywhere(*sums, gram_ref, sum_peers, sems, copies, meanwhile)
    for copy in copies:
        copy.wait_send()


def partners():
    x, y, z, core = place()
    return (
        [device(lax.rem(x + d, 4), y, z, core) for d in (1, 2, 3)],
        [device(x, lax.rem(y + d, 4), z, core) for d in (1, 2, 3)],
        [device(x, y, lax.rem(z + d, 8), core) for d in range(1, 8)],
        [device(x, y, z, 1 - core)],
    )


def sum_everywhere(packed, r1, a1, ra, rb, a2, b2, ra2, rb2, zbuf, gbuf, peers, sems, copies, meanwhile):
    x, y, z, core = place()
    x_peers, y_peers, z_peers, core_peers = peers

    def spread(group, piece):
        started = [send(*piece(d), *sems(), peer) for d, peer in enumerate(group)]
        copies.extend(started)
        return started

    def arrived(started):
        for copy in started:
            copy.wait_recv()

    def total(own, parts):
        return (own + parts[0]) + (parts[1] + parts[2])

    def one(source, target, peer):
        copies.append(send(source, target, *sems(), peer))
        return copies[-1]

    def piece_a(d):
        return lax.rem(x + d, 4) * 96

    def piece_b(d):
        return 384 + lax.rem(y + d, 4) * 64

    pieces = [(piece_a(d), 96, x_peers, ra, d) for d in (1, 2, 3, 0)], [(piece_b(d), 64, y_peers, rb, d) for d in (1, 2, 3, 0)]
    pieces = [piece for pair in zip(*pieces) for piece in pair]
    landing = [
        one(packed.at[rows_at((1 - core) * 640 + at, size)], r1.at[rows_at(at, size)], core_peers[0])
        for at, size, _, _, _ in pieces
    ]
    started = []
    for copy, (at, size, group, target, d) in zip(landing, pieces):
        copy.wait_recv()
        a1[rows_at(at, size)] = packed[rows_at(core * 640 + at, size)] + r1[rows_at(at, size)]
        if d > 0:
            started.append(one(a1.at[rows_at(at, size)], target.at[d - 1], group[d - 1]))
    meanwhile()
    arrived(started)
    a2[...] = total(a1[rows_at(x * 96, 96)], ra)
    b2[...] = total(a1[rows_at(384 + y * 64, 64)], rb)
    started = spread(y_peers, lambda d: (a2.at[rows_at(lax.rem(y + d + 1, 4) * 24, 24)], ra2.at[d]))
    started += spread(x_peers, lambda d: (b2.at[rows_at(lax.rem(x + d + 1, 4) * 16, 16)], rb2.at[d]))
    arrived(started)
    zbuf[z, :24] = total(a2[rows_at(y * 24, 24)], ra2)
    zbuf[z, 24:] = total(b2[rows_at(x * 16, 16)], rb2)
    arrived(spread(z_peers, lambda d: (zbuf.at[z], zbuf.at[z])))
    whole = ((zbuf[0] + zbuf[1]) + (zbuf[2] + zbuf[3])) + ((zbuf[4] + zbuf[5]) + (zbuf[6] + zbuf[7]))
    own_a = rows_at(core * 640 + x * 96 + y * 24, 24)
    own_b = rows_at(core * 640 + 384 + y * 64 + x * 16, 16)
    gbuf[own_a] = whole[:24]
    gbuf[own_b] = whole[24:]
    started = spread(y_peers, lambda d: (gbuf.at[own_a], gbuf.at[own_a]))
    started += spread(x_peers, lambda d: (gbuf.at[own_b], gbuf.at[own_b]))
    arrived(started)

    def share(at, size, peer):
        rows = rows_at(core * 640 + at, size)
        return one(gbuf.at[rows], gbuf.at[rows], peer)

    started = []
    for d in range(3):
        started.append((share(x * 96, 96, x_peers[d]), piece_a(3 - d), 96))
        started.append((share(384 + y * 64, 64, y_peers[d]), piece_b(3 - d), 64))
    landing = [share(x * 96, 96, core_peers[0]), share(384 + y * 64, 64, core_peers[0])]
    for copy, at, size in started:
        copy.wait_recv()
        landing.append(share(at, size, core_peers[0]))
    arrived(landing)


def filtered_rows(start_states, couplings, potential, site_offsets, coupling_index, degrees):
    vmem, smem = pl.BlockSpec(memory_space=pltpu.VMEM), pl.BlockSpec(memory_space=pltpu.SMEM)
    scratch = [pltpu.VMEM((2, 16, WIDTH, 128), F32)] * (3 * NCH)
    scratch += [pltpu.VMEM((2, 16, 2 * WIDTH, 128), BF16)] * (3 * NCH)
    for k in range(3):
        for c in range(NCH):
            scratch += [pltpu.VMEM((16, WIDTH // parts_of(k, c), 128), F32)] * (2 * parts_of(k, c))
    scratch += [pltpu.VMEM((2, 16, WIDTH, 128), F32)] * NCH
    scratch += [pltpu.VMEM((16, 2, WIDTH, 128), F32)] * NCH
    scratch += [pltpu.VMEM((16, 128, 256), BF16), pltpu.VMEM((16, 128), F32), pltpu.VMEM((16, 128), F32)]
    scratch += [pltpu.VMEM((8, 16, 128), F32)] * 2
    scratch += [pltpu.VMEM((128, 128), jnp.int32)]
    scratch += [pltpu.VMEM((4, 2, 512, 128), F32), pltpu.VMEM((1280, 128), F32)]
    scratch += [pltpu.VMEM((640, 128), F32), pltpu.VMEM((640, 128), F32)]
    scratch += [pltpu.VMEM((3, 96, 128), F32), pltpu.VMEM((3, 64, 128), F32)]
    scratch += [pltpu.VMEM((96, 128), F32), pltpu.VMEM((64, 128), F32)]
    scratch += [pltpu.VMEM((3, 24, 128), F32), pltpu.VMEM((3, 16, 128), F32), pltpu.VMEM((8, 40, 128), F32)]
    scratch += [pltpu.SemaphoreType.DMA((COPIES,))] * 2
    return pl.pallas_call(
        filter_kernel,
        out_shape=[
            jax.ShapeDtypeStruct((1280, 128), F32),
            jax.ShapeDtypeStruct((1024, 512), BF16),
            jax.ShapeDtypeStruct((1024, 512), BF16),
        ],
        in_specs=[smem, smem, vmem, vmem, vmem, vmem],
        out_specs=[vmem] * 3,
        scratch_shapes=scratch,
        compiler_params=pltpu.CompilerParams(collective_id=0, has_side_effects=True, vmem_limit_bytes=VMEM_LIMIT),
        name="filter",
    )(coupling_index.transpose(1, 0, 2), site_offsets.transpose(1, 0, 2), start_states, couplings, potential, degrees.reshape(1, 128))


def per_device(start_states, couplings, potential, site_offsets, coupling_index, degrees):
    gram, xh, xl = filtered_rows(start_states, couplings, potential, site_offsets, coupling_index, degrees)
    return orthonormalised(gram, xh, xl).reshape(2, 4, 128, 512)


def solution(mesh):
    in_specs = (
        P("blk", None, None, "states"),
        P(),
        P("blk", None, None),
        P("blk", None, None),
        P("blk", None, None),
        P("states"),
    )
    out_specs = P("blk", "states", None, None)
    return jax.shard_map(
        per_device, mesh=mesh, in_specs=in_specs, out_specs=out_specs, check_vma=False
    )
```
